32 devices in a mesh: depth: 4 (over y, core), tile: 8 (over z, x).
Axes of the slice: x: 2, y: 2, z: 4, core: 2. Of those that a mesh axis runs over, the one named last changes fastest.
Arguments:
- volume: bfloat16 [128, 18, 512], P(('depth', 'tile')), may hold values from -6 to 6
- ray_entry: int32 [16, 512], P(None, 'tile'), may hold values from 0 to 63
- ray_exit: int32 [16, 512], P(None, 'tile'), may hold values from 64 to 128
- palette: float32 [3, 2], replicated, may hold values from -2 to 2
- light_dir: float32 [3], replicated, may hold values from -3 to 3
Outputs:
- layers: float32 [4, 4, 16, 512], P('depth', None, None, 'tile')
The draws below stay inside these ranges and needn't reach their ends.
All inputs are finite; a program needn't handle non-finite values.
Results may differ from the reference program's by a relative error of at most 0.0003.
Values may be sent and summed in bfloat16 or wider, within the bound.
No kernel may reach another device: no remote copies, remote signals or barrier semaphores. Data moves between devices by JAX's collectives and lax.ppermute only.
A program may use at most 64 MiB of HBM per device.

```python
import jax
import jax.numpy as jnp
from jax import lax

ROWS = 16
SLAB = 32
DEPTH_TOTAL = 128
COLS = 512
N_DEPTH = 4


def touch_ends(drawn, stream_key, least, largest):
    dims = drawn.shape
    place = [jax.random.randint(jax.random.fold_in(stream_key, axis), (), 0, dims[axis]) for axis in range(len(dims))]
    drawn = drawn.at[tuple(place)].set(least)
    longest = dims.index(max(dims))
    place[longest] = (place[longest] + 1) % dims[longest]
    return drawn.at[tuple(place)].set(largest)


def block_scale(stream_key, extent, pieces, smallest, high):
    def one(dim, parts):
        steps = jax.random.uniform(jax.random.fold_in(jax.random.fold_in(stream_key, 6), dim), (parts,), jnp.float32, smallest / len(pieces), high / len(pieces))
        return jnp.repeat(jnp.exp(steps), extent[dim] // parts).reshape((-1,) + (1,) * (len(extent) - dim - 1))

    gain = one(*pieces[0])
    for cut in pieces[1:]:
        gain = gain * one(*cut)
    return gain


def gaussian(own_key, shape, spread, reach, cuts=(), kind=jnp.bfloat16):
    entries = spread * jax.random.normal(own_key, shape, jnp.float32)
    if cuts:
        entries = entries * block_scale(own_key, shape, cuts, -0.22, 0.18)
    return jnp.clip(entries, -reach, reach).astype(kind)


def setup_inputs(seed: int = 0) -> dict:
    seeds = jax.random.split(jax.random.key(seed), 6)
    volume = gaussian(seeds[0], (DEPTH_TOTAL, ROWS + 2, COLS), 1.0, 6.0, ((0, 32),))
    ray_entry = touch_ends(jax.random.randint(seeds[1], (ROWS, COLS), 0, DEPTH_TOTAL // 2), jax.random.fold_in(seeds[1], 1), 0, (DEPTH_TOTAL // 2) - 1).astype(jnp.int32)
    ray_exit = touch_ends(jax.random.randint(seeds[2], (ROWS, COLS), DEPTH_TOTAL // 2, DEPTH_TOTAL + 1), jax.random.fold_in(seeds[2], 1), DEPTH_TOTAL // 2, DEPTH_TOTAL).astype(jnp.int32)
    palette = jnp.clip(jax.random.uniform(seeds[3], (3, 2), jnp.float32, -2.0, 2.0), -2.0, 2.0)
    light_dir = gaussian(seeds[4], (3,), 1.0, 3.0, (), jnp.float32)
    return dict(volume=volume, ray_entry=ray_entry, ray_exit=ray_exit, palette=palette, light_dir=light_dir)


def shade_slab(brick_block, ray_entry, ray_exit, palette, light_dir, first_sample, total_depth):
    values = brick_block.astype(jnp.float32)
    grad_depth = (values[2:, 1:-1, 1:-1] - values[:-2, 1:-1, 1:-1]) * 0.5
    grad_rows = (values[1:-1, 2:, 1:-1] - values[1:-1, :-2, 1:-1]) * 0.5
    grad_cols = (values[1:-1, 1:-1, 2:] - values[1:-1, 1:-1, :-2]) * 0.5
    sample = values[1:-1, 1:-1, 1:-1]
    facing = grad_depth * light_dir[0] + grad_rows * light_dir[1] + grad_cols * light_dir[2]
    length = jnp.sqrt(grad_depth * grad_depth + grad_rows * grad_rows + grad_cols * grad_cols + 1.0)
    shading = 0.3 + 0.7 * jnp.abs(facing) / length
    position = first_sample + lax.broadcasted_iota(jnp.int32, sample.shape, 0)
    inside = (position >= ray_entry[None]) & (position < ray_exit[None])
    excess = jnp.maximum(sample - 1.5, 0.0)
    optical = jnp.where(inside, excess * excess * (64.0 / total_depth), 0.0)
    before = jnp.cumsum(optical, axis=0) - optical
    weight = jnp.exp(-before) * (1.0 - jnp.exp(-optical))
    colours = []
    for channel in range(3):
        tint = jax.nn.sigmoid(palette[channel, 0] * sample + palette[channel, 1])
        colours.append(lax.optimization_barrier(jnp.sum(weight * tint * shading, axis=0)))
    colour = jnp.stack(colours)
    transmit = jnp.exp(-lax.optimization_barrier(jnp.sum(optical, axis=0)))
    return (colour, transmit)

def reference(volume, ray_entry, ray_exit, palette, light_dir):
    padded = jnp.pad(volume, ((1, 1), (0, 0), (1, 1)))
    total_depth = SLAB * N_DEPTH

    def per_slab(carry, index):
        start = (index * SLAB).astype(jnp.int32)
        brick_block = lax.dynamic_slice(padded, (start, jnp.int32(0), jnp.int32(0)), (SLAB + 2, ROWS + 2, COLS + 2))
        colour, transmit = shade_slab(brick_block, ray_entry, ray_exit, palette, light_dir, start, total_depth)
        new_colour = carry[0] + carry[1][None] * colour
        new_transmit = carry[1] * transmit
        layer = jnp.concatenate([new_colour, new_transmit[None]], 0)
        return ((new_colour, new_transmit), layer)
    init = (jnp.zeros((3, ROWS, COLS), jnp.float32), jnp.ones((ROWS, COLS), jnp.float32))
    _, layers = lax.scan(per_slab, init, jnp.arange(N_DEPTH, dtype=jnp.int32))
    return layers
```

```python
import functools
import math

import jax
import jax.numpy as jnp
from jax import lax
from jax.experimental import pallas as pl
from jax.experimental.pallas import tpu as pltpu
from jax.sharding import PartitionSpec as P

LANES = 128
VMEM = pltpu.VMEM
SMEM = pltpu.SMEM
F32 = jnp.float32
PLANES = 14


def lane_index(rows):
    return lax.broadcasted_iota(jnp.int32, (rows, LANES), 1)


def pack_kernel(col_dev, cells_ref, chunk_ref):
    rows_two, depth_sub, columns = cells_ref.shape
    tiles = columns // col_dev
    per = LANES // col_dev
    blocks = columns // LANES
    lane = lax.broadcasted_iota(jnp.int32, (rows_two, depth_sub, LANES), 2)

    def block(index):
        if index < 0 or index >= blocks:
            return jnp.zeros((rows_two, depth_sub, LANES), F32)
        return cells_ref[:, :, index * LANES:(index + 1) * LANES].astype(F32)

    for tile in range(tiles):
        own, place = tile // per, (tile % per) * col_dev
        here = block(own)
        if place == 0:
            left = block(own - 1)
            chunk = jnp.where(lane == LANES - 1, left, here)
        else:
            right = block(own + 1)
            chunk = pltpu.roll(here, LANES - place, 2)
            chunk = jnp.where(lane == col_dev, pltpu.roll(right, LANES - place, 2), chunk)
        chunk_ref[tile] = chunk.astype(chunk_ref.dtype)


def shade(facing, square):
    return 0.3 + jnp.abs(facing) * lax.rsqrt(square)


def slab_kernel(depth_sub, rows, optical_scale, where_ref, palette_ref, light_ref, chunk_ref, entry_ref, exit_ref, out_ref, cells):
    tiles, per_chunk, _ = chunk_ref.shape
    col_dev = entry_ref.shape[1]
    rows_two = per_chunk // depth_sub
    first_sample = where_ref[0] * (depth_sub * tiles)
    light = [light_ref[axis] * 0.7 for axis in range(3)]
    slope = [palette_ref[ch, 0] * 0.5 for ch in range(3)]
    offset = [palette_ref[ch, 1] * 0.5 for ch in range(3)]
    scale = optical_scale * math.log2(math.e)

    def widen(tile):
        cells[pl.ds(tile * per_chunk, per_chunk), :] = chunk_ref[tile].astype(F32)

    if tiles <= 8:
        for tile in range(tiles):
            widen(tile)
    else:
        lax.fori_loop(0, tiles, lambda tile, nothing: (widen(tile), nothing)[1], 0)

    low = lane_index(8) < col_dev

    def pair(one, other):
        return jnp.where(low, one, pltpu.roll(other, col_dev, 1))

    for half in range(rows // 8):
        top = half * 8
        entry = entry_ref[top:top + 8, :] - first_sample
        leave = exit_ref[top:top + 8, :] - first_sample
        fill = jnp.zeros((8, LANES - col_dev), jnp.int32)
        entry = jnp.concatenate([entry, fill], axis=1)
        leave = jnp.concatenate([leave, fill], axis=1)

        def load(tile, sub, row):
            return cells[pl.ds(tile * per_chunk + (top + 1 + row) * depth_sub + sub, 8, stride=depth_sub), :]

        def flat(tile, sub, here):
            rise_row = load(tile, sub, 1) - load(tile, sub, -1)
            rise_col = pltpu.roll(here, LANES - 1, 1) - pltpu.roll(here, 1, 1)
            facing = rise_row * light[1] + rise_col * light[2]
            square = rise_row * rise_row + rise_col * rise_col + 4.0
            return facing, square

        def sample(tile, sub, here, before, passed):
            index = tile * depth_sub + sub
            inside = (entry <= index) & (leave > index)
            excess = jnp.maximum(here - 1.5, 0.0)
            optical = jnp.where(inside, excess * excess * scale, 0.0)
            before = before + optical
            left = jnp.exp2(-before)
            return before, left, passed - left

        def chunk(tile, carry, first=False, last=False):
            before, passed, prev, here, white, tinted = carry
            kept = []
            for sub in range(depth_sub):
                final = last and sub == depth_sub - 1
                if final:
                    after = here
                else:
                    after = load(tile + (sub + 1) // depth_sub, (sub + 1) % depth_sub, 0)
                before, passed, weight = sample(tile, sub, here, before, passed)
                facing, square = flat(tile, sub, here)
                if first and sub == 0:
                    kept = [here, after, facing, square, weight]
                elif final:
                    kept = [here, prev, facing, square, weight]
                else:
                    rise = after - prev
                    lit = weight * shade(facing + rise * light[0], square + rise * rise)
                    white = white + lit
                    tinted = [tinted[ch] + lit * jnp.tanh(here * slope[ch] + offset[ch]) for ch in range(3)]
                prev, here = here, after
            return (before, passed, prev, here, white, tinted), kept

        zero = jnp.zeros((8, LANES), F32)
        start = load(0, 0, 0)
        carry = (zero, zero + 1.0, start, start, zero, [zero] * 3)
        carry, near = chunk(0, carry, first=True)
        if tiles <= 8:
            for tile in range(1, tiles - 1):
                carry, _ = chunk(tile, carry)
        else:
            carry = lax.fori_loop(1, tiles - 1, lambda tile, now: chunk(tile, now)[0], carry)
        carry, far = chunk(tiles - 1, carry, last=True)
        before, passed, _, _, white, tinted = carry
        planes = [0.5 * (white + tinted[ch]) for ch in range(3)] + [passed] + near + far
        for index in range(PLANES // 2):
            out_ref[index, top:top + 8, :] = pair(planes[2 * index], planes[2 * index + 1])


def layer_kernel(slabs, rows, where_ref, palette_ref, light_ref, planes_ref, out_ref):
    col_dev = out_ref.shape[3]
    mine = where_ref[0]
    light = light_ref[0] * 0.7
    slope = [palette_ref[ch, 0] * 0.5 for ch in range(3)]
    offset = [palette_ref[ch, 1] * 0.5 for ch in range(3)]

    for half in range(rows // 8):
        top = half * 8

        def plane(slab, index):
            held = planes_ref[slab, index // 2, top:top + 8, :]
            return pltpu.roll(held, col_dev, 1) if index % 2 else held

        def bound(slab, at, rise):
            here = plane(slab, at)
            lit = 0.5 * plane(slab, at + 4) * shade(
                plane(slab, at + 2) + rise * light, plane(slab, at + 3) + rise * rise
            )
            return [lit + lit * jnp.tanh(here * slope[ch] + offset[ch]) for ch in range(3)]

        def step(slab, carry):
            colour, passed = carry
            zero = jnp.zeros((8, LANES), F32)
            ahead = jnp.where(slab > 0, plane(jnp.maximum(slab - 1, 0), 9), zero)
            behind = jnp.where(slab < slabs - 1, plane(jnp.minimum(slab + 1, slabs - 1), 4), zero)
            near = bound(slab, 4, plane(slab, 5) - ahead)
            far = bound(slab, 9, behind - plane(slab, 10))
            colour = [colour[ch] + passed * (plane(slab, ch) + near[ch] + far[ch]) for ch in range(3)]
            return colour, passed * plane(slab, 3)

        zero = jnp.zeros((8, LANES), F32)
        colour, passed = lax.fori_loop(0, mine + 1, step, ([zero] * 3, zero + 1.0))
        for ch in range(3):
            out_ref[0, ch, top:top + 8, :] = colour[ch][:, :col_dev]
        out_ref[0, 3, top:top + 8, :] = passed[:, :col_dev]


def body(volume, ray_entry, ray_exit, palette, light_dir):
    tiles = lax.axis_size("tile")
    slabs = lax.axis_size("depth")
    depth_sub, rows_two, columns = volume.shape
    rows, col_dev = ray_entry.shape
    total = depth_sub * tiles * slabs
    vmem = pl.BlockSpec(memory_space=VMEM)
    smem = pl.BlockSpec(memory_space=SMEM)
    where = lax.axis_index("depth").astype(jnp.int32).reshape(1)

    chunks = pl.pallas_call(
        functools.partial(pack_kernel, col_dev),
        out_shape=jax.ShapeDtypeStruct((tiles, rows_two, depth_sub, LANES), volume.dtype),
        in_specs=[vmem],
        out_specs=vmem,
        name="pack",
    )(jnp.transpose(volume, (1, 0, 2)))
    chunks = chunks.reshape(tiles, rows_two * depth_sub, LANES)
    slab = lax.all_to_all(chunks, "tile", split_axis=0, concat_axis=0, tiled=True)
    planes = pl.pallas_call(
        functools.partial(slab_kernel, depth_sub, rows, 64.0 / total),
        out_shape=jax.ShapeDtypeStruct((PLANES // 2, rows, LANES), F32),
        in_specs=[smem, smem, smem, vmem, vmem, vmem],
        out_specs=vmem,
        scratch_shapes=[pltpu.VMEM((tiles * rows_two * depth_sub, LANES), F32)],
        name="slab",
    )(where, palette, light_dir, slab, ray_entry, ray_exit)
    planes = lax.all_gather(planes, "depth")
    return pl.pallas_call(
        functools.partial(layer_kernel, slabs, rows),
        out_shape=jax.ShapeDtypeStruct((1, 4, rows, col_dev), F32),
        in_specs=[smem, smem, smem, vmem],
        out_specs=vmem,
        name="layer",
    )(where, palette, light_dir, planes)


def solution(mesh):
    return jax.shard_map(
        body,
        mesh=mesh,
        in_specs=(P(("depth", "tile"), None, None), P(None, "tile"), P(None, "tile"), P(), P()),
        out_specs=P("depth", None, None, "tile"),
        check_vma=False,
    )
```

```python
import functools
import math

import jax
import jax.numpy as jnp
from jax import lax
from jax.experimental import pallas as pl
from jax.experimental.pallas import tpu as pltpu
from jax.sharding import PartitionSpec as P

LANES = 128
VMEM = pltpu.VMEM
F32 = jnp.float32
PLANES = 14


def lane_index(rows):
    return lax.broadcasted_iota(jnp.int32, (rows, LANES), 1)


def pack_kernel(col_dev, cells_ref, chunk_ref):
    rows_two, depth_sub, columns = cells_ref.shape
    tiles = columns // col_dev
    per = LANES // col_dev
    blocks = columns // LANES
    lane = lax.broadcasted_iota(jnp.int32, (rows_two, depth_sub, LANES), 2)

    def block(index):
        if index < 0 or index >= blocks:
            return jnp.zeros((rows_two, depth_sub, LANES), F32)
        return cells_ref[:, :, index * LANES:(index + 1) * LANES].astype(F32)

    for tile in range(tiles):
        own, place = tile // per, (tile % per) * col_dev
        here = block(own)
        if place == 0:
            left = block(own - 1)
            chunk = jnp.where(lane == LANES - 1, left, here)
        else:
            right = block(own + 1)
            chunk = pltpu.roll(here, LANES - place, 2)
            chunk = jnp.where(lane == col_dev, pltpu.roll(right, LANES - place, 2), chunk)
        chunk_ref[tile] = chunk.astype(chunk_ref.dtype)


def shade(facing, square):
    return 0.3 + jnp.abs(facing) * lax.rsqrt(square)


def settings(setting_ref):
    slope = [setting_ref[ch] for ch in range(3)]
    offset = [setting_ref[3 + ch] for ch in range(3)]
    light = [setting_ref[6 + axis] for axis in range(3)]
    return slope, offset, light


def slab_kernel(depth_sub, rows, col_dev, optical_scale, setting_ref, span_ref, chunk_ref, out_ref, cells):
    tiles, per_chunk, _ = chunk_ref.shape
    slope, offset, light = settings(setting_ref)
    scale = optical_scale * math.log2(math.e)

    def widen(tile):
        cells[pl.ds(tile * per_chunk, per_chunk), :] = chunk_ref[tile].astype(F32)

    if tiles <= 8:
        for tile in range(tiles):
            widen(tile)
    else:
        lax.fori_loop(0, tiles, lambda tile, nothing: (widen(tile), nothing)[1], 0)

    low = lane_index(8) < col_dev

    def pair(one, other):
        return jnp.where(low, one, pltpu.roll(other, col_dev, 1))

    for half in range(rows // 8):
        top = half * 8
        entry = span_ref[0, top:top + 8, :]
        leave = span_ref[1, top:top + 8, :]

        def load(tile, sub, row):
            return cells[pl.ds(tile * per_chunk + (top + 1 + row) * depth_sub + sub, 8, stride=depth_sub), :]

        def flat(tile, sub, here):
            rise_row = load(tile, sub, 1) - load(tile, sub, -1)
            rise_col = pltpu.roll(here, LANES - 1, 1) - pltpu.roll(here, 1, 1)
            facing = rise_row * light[1] + rise_col * light[2]
            square = rise_row * rise_row + rise_col * rise_col + 4.0
            return facing, square

        def sample(tile, sub, here, before, passed):
            index = tile * depth_sub + sub
            inside = (entry <= index) & (leave > index)
            excess = jnp.maximum(here - 1.5, 0.0)
            optical = jnp.where(inside, excess * excess * scale, 0.0)
            before = before + optical
            left = jnp.exp2(-before)
            return before, left, passed - left

        def chunk(tile, carry, first=False, last=False):
            before, passed, prev, here, white, tinted = carry
            kept = []
            for sub in range(depth_sub):
                final = last and sub == depth_sub - 1
                if final:
                    after = here
                else:
                    after = load(tile + (sub + 1) // depth_sub, (sub + 1) % depth_sub, 0)
                before, passed, weight = sample(tile, sub, here, before, passed)
                facing, square = flat(tile, sub, here)
                if first and sub == 0:
                    kept = [here, after, facing, square, weight]
                elif final:
                    kept = [here, prev, facing, square, weight]
                else:
                    rise = after - prev
                    lit = weight * shade(facing + rise * light[0], square + rise * rise)
                    white = white + lit
                    tinted = [tinted[ch] + lit * jnp.tanh(here * slope[ch] + offset[ch]) for ch in range(3)]
                prev, here = here, after
            return (before, passed, prev, here, white, tinted), kept

        zero = jnp.zeros((8, LANES), F32)
        start = load(0, 0, 0)
        carry = (zero, zero + 1.0, start, start, zero, [zero] * 3)
        carry, near = chunk(0, carry, first=True)
        if tiles <= 8:
            for tile in range(1, tiles - 1):
                carry, _ = chunk(tile, carry)
        else:
            carry = lax.fori_loop(1, tiles - 1, lambda tile, now: chunk(tile, now)[0], carry)
        carry, far = chunk(tiles - 1, carry, last=True)
        before, passed, _, _, white, tinted = carry
        planes = [0.5 * (white + tinted[ch]) for ch in range(3)] + [passed] + near + far
        for index in range(PLANES // 2):
            out_ref[index, top:top + 8, :] = pair(planes[2 * index], planes[2 * index + 1])


def layer_kernel(slabs, rows, setting_ref, planes_ref, out_ref):
    col_dev = out_ref.shape[3]
    slope, offset, (light, _, _) = settings(setting_ref)
    mine = setting_ref[9]

    for half in range(rows // 8):
        top = half * 8

        def plane(slab, index):
            held = planes_ref[slab, index // 2, top:top + 8, :]
            return pltpu.roll(held, col_dev, 1) if index % 2 else held

        def bound(slab, at, rise):
            here = plane(slab, at)
            lit = 0.5 * plane(slab, at + 4) * shade(
                plane(slab, at + 2) + rise * light, plane(slab, at + 3) + rise * rise
            )
            return [lit + lit * jnp.tanh(here * slope[ch] + offset[ch]) for ch in range(3)]

        def step(slab, carry):
            colour, passed = carry
            reached = jnp.where(mine >= jnp.asarray(slab, F32), passed, 0.0)
            zero = jnp.zeros((8, LANES), F32)
            if isinstance(slab, int):
                ahead = plane(slab - 1, 9) if slab > 0 else zero
                behind = plane(slab + 1, 4) if slab < slabs - 1 else zero
            else:
                ahead = jnp.where(slab > 0, plane(jnp.maximum(slab - 1, 0), 9), zero)
                behind = jnp.where(slab < slabs - 1, plane(jnp.minimum(slab + 1, slabs - 1), 4), zero)
            near = bound(slab, 4, plane(slab, 5) - ahead)
            far = bound(slab, 9, behind - plane(slab, 10))
            colour = [colour[ch] + reached * (plane(slab, ch) + near[ch] + far[ch]) for ch in range(3)]
            return colour, jnp.where(mine >= jnp.asarray(slab, F32), passed * plane(slab, 3), passed)

        zero = jnp.zeros((8, LANES), F32)
        carry = ([zero] * 3, zero + 1.0)
        if slabs <= 4:
            for slab in range(slabs):
                carry = step(slab, carry)
        else:
            carry = lax.fori_loop(0, slabs, step, carry)
        colour, passed = carry
        for ch in range(3):
            out_ref[0, ch, top:top + 8, :] = colour[ch][:, :col_dev]
        out_ref[0, 3, top:top + 8, :] = passed[:, :col_dev]


def body(volume, ray_entry, ray_exit, palette, light_dir):
    tiles = lax.axis_size("tile")
    slabs = lax.axis_size("depth")
    depth_sub, rows_two, columns = volume.shape
    rows, col_dev = ray_entry.shape
    total = depth_sub * tiles * slabs
    vmem = pl.BlockSpec(memory_space=VMEM)
    resident = functools.partial(pltpu.with_memory_space_constraint, memory_space=VMEM)
    where = lax.axis_index("depth").astype(jnp.int32)

    scalars = jnp.concatenate(
        [palette[:, 0] * 0.5, palette[:, 1] * 0.5, light_dir * 0.7, where.astype(F32)[None]]
    )
    setting = resident(jnp.broadcast_to(scalars[:, None, None], (10, 8, LANES)))
    span = jnp.stack([ray_entry, ray_exit]) - where * (depth_sub * tiles)
    span = resident(jnp.pad(span, ((0, 0), (0, 0), (0, LANES - col_dev))))

    chunks = pl.pallas_call(
        functools.partial(pack_kernel, col_dev),
        out_shape=pltpu.VMEM((tiles, rows_two, depth_sub, LANES), volume.dtype),
        in_specs=[vmem],
        out_specs=vmem,
        name="pack",
    )(jnp.transpose(volume, (1, 0, 2)))
    chunks = chunks.reshape(tiles, rows_two * depth_sub, LANES)
    slab = lax.all_to_all(chunks, "tile", split_axis=0, concat_axis=0, tiled=True)
    planes = pl.pallas_call(
        functools.partial(slab_kernel, depth_sub, rows, col_dev, 64.0 / total),
        out_shape=pltpu.VMEM((PLANES // 2, rows, LANES), F32),
        in_specs=[vmem, vmem, vmem],
        out_specs=vmem,
        scratch_shapes=[pltpu.VMEM((tiles * rows_two * depth_sub, LANES), F32)],
        name="slab",
    )(setting, span, resident(slab))
    planes = lax.all_gather(planes, "depth")
    return pl.pallas_call(
        functools.partial(layer_kernel, slabs, rows),
        out_shape=jax.ShapeDtypeStruct((1, 4, rows, col_dev), F32),
        in_specs=[vmem, vmem],
        out_specs=vmem,
        name="layer",
    )(setting, resident(planes))


def solution(mesh):
    return jax.shard_map(
        body,
        mesh=mesh,
        in_specs=(P(("depth", "tile"), None, None), P(None, "tile"), P(None, "tile"), P(), P()),
        out_specs=P("depth", None, None, "tile"),
        check_vma=False,
    )
```

```python
import functools
import math

import jax
import jax.numpy as jnp
from jax import lax
from jax.experimental import pallas as pl
from jax.experimental.pallas import tpu as pltpu
from jax.sharding import PartitionSpec as P

LANES = 128
GROUP = 32
PER = LANES // GROUP
CHUNK = 24
UNIT = 32
SHORT = 8
VMEM = pltpu.VMEM
F32 = jnp.float32


def turn(cells, by):
    return pltpu.roll(cells, by % LANES, 1)


def slide(cells, by):
    return pltpu.roll(cells, by % 8, 0)


def places():
    sub = lax.broadcasted_iota(jnp.int32, (8, LANES), 0)
    lane = lax.broadcasted_iota(jnp.int32, (8, LANES), 1)
    return sub, lane // GROUP, lane % GROUP


def exchange(rows, group):
    low, even = group < 2, group % 2 == 0
    left = [jnp.where(low, rows[i], turn(rows[i + 2], 2 * GROUP)) for i in range(2)]
    right = [jnp.where(low, turn(rows[i], -2 * GROUP), rows[i + 2]) for i in range(2)]
    out = []
    for one, two in (left, right):
        out.append(jnp.where(even, one, turn(two, GROUP)))
        out.append(jnp.where(even, turn(one, -GROUP), two))
    return out


def pack_kernel(slabs, cells_ref, chunk_ref, staged):
    rows_two, depth_sub, columns = cells_ref.shape
    blocks = columns // LANES
    tiles = columns // (2 * GROUP)
    flat = rows_two * depth_sub
    sub, group, col = places()
    lead = 7 * depth_sub
    for block in range(blocks):
        part = cells_ref[:, :, block * LANES:(block + 1) * LANES].astype(F32)
        staged[block, lead:lead + flat, :] = part.reshape(flat, LANES)

    def rows_of(block, sub_sample, row):
        return staged[block, pl.ds(lead + row * depth_sub + sub_sample, 8, stride=depth_sub), :]

    ready = {}

    def half_tile(index):
        if index < 0 or index >= blocks * PER:
            return [jnp.zeros((8, LANES), F32)] * 3
        block = index // PER
        if block not in ready:
            first = [rows_of(block, s, 1) for s in range(depth_sub)]
            second = [rows_of(block, s, 9) for s in range(depth_sub)]
            outer = [
                jnp.where(sub == 7, rows_of(block, s, -7), rows_of(block, s, rows_two - 1))
                for s in range(depth_sub)
            ]
            ready[block] = [exchange(part, group) for part in (first, second, outer)]
        return [part[index % PER] for part in ready[block]]

    for index in range(blocks * PER):
        before, here, after = (half_tile(index + step) for step in (-1, 0, 1))
        edge = [
            jnp.where(col == 0, turn(before[a], 1 - GROUP), turn(after[a], GROUP - 1))
            for a in range(2)
        ]
        second = jnp.where(col == 1, turn(edge[1], 1), turn(edge[1], -1))
        rest = jnp.where(
            sub == 1,
            slide(edge[0], 1),
            jnp.where(sub == 6, slide(edge[0], -1), jnp.where(sub == 2, slide(edge[1], 2), slide(edge[1], -2))),
        )
        rest = jnp.where(col == 2, turn(rest, 2), turn(rest, -2))
        halo = jnp.where(
            (col == 0) | (col == GROUP - 1), edge[0], jnp.where((col == 1) | (col == GROUP - 2), second, rest)
        )
        outer = jnp.where((sub == 0) | (sub == 7), here[2], halo)
        chunk = jnp.concatenate([here[0], here[1], outer], axis=0).astype(chunk_ref.dtype)
        for slab in range(index % 2, slabs, 2):
            chunk_ref[slab * tiles + index // 2] = chunk


def ray_kernel(tiles, slabs, optical_scale, setting_ref, span_ref, chunk_ref, mine_ref, other_ref, cells, slopes):
    depth_sub = PER
    slab_len = tiles * depth_sub
    slope = [setting_ref[ch] for ch in range(3)]
    offset = [setting_ref[3 + ch] for ch in range(3)]
    light = [setting_ref[6 + axis] for axis in range(3)]
    target = [setting_ref[9], setting_ref[10]]
    scale = optical_scale * math.log2(math.e)
    sub, group, col = places()
    zero = jnp.zeros((8, LANES), F32)
    unroll = tiles <= SHORT

    def each(count, step, carry):
        if unroll:
            for index in range(count):
                carry = step(index, carry)
            return carry
        return lax.fori_loop(0, count, step, carry)

    def spread(base):
        def step(tile, nothing):
            wide = [chunk_ref[(base + k) * tiles + tile].astype(F32) for k in range(PER)]
            first, second, outer = (
                exchange([part[8 * a:8 * a + 8] for part in wide], group) for a in range(3)
            )
            for s in range(depth_sub):
                at = (tile * depth_sub + s) * UNIT
                flank = outer[s]
                two = jnp.where(col == 0, turn(flank, -1), turn(flank, 1))
                rest = jnp.where(col == 0, turn(flank, -2), turn(flank, 2))
                inner = (sub > 0) & (sub < 7)
                edge = [
                    jnp.where(inner, flank, jnp.where(sub == 0, slide(rest, -1), slide(rest, 1))),
                    jnp.where(inner, two, jnp.where(sub == 0, slide(rest, -2), slide(rest, 2))),
                ]
                cells[pl.ds(at, 8), :] = flank
                cells[pl.ds(at + 24, 8), :] = flank
                for a, here in ((0, first[s]), (1, second[s])):
                    cells[pl.ds(at + 8 + 8 * a, 8), :] = here
                    rise = jnp.where(col == GROUP - 1, edge[a], turn(here, -1)) - jnp.where(
                        col == 0, edge[a], turn(here, 1)
                    )
                    slopes[pl.ds((tile * depth_sub + s) * 16 + 8 * a, 8), :] = rise
            return nothing

        each(tiles, step, 0)

    def march(base, half, ahead, behind):
        top = 8 + 8 * half
        entry = span_ref[0, 8 * half:8 * half + 8, :] - base * slab_len
        leave = span_ref[1, 8 * half:8 * half + 8, :] - base * slab_len

        def load(index, shift=0):
            return cells[pl.ds(index * UNIT + top + shift, 8), :]

        def sample(index, after, carry):
            before, passed, prev, here, white, tinted = carry
            inside = (entry <= index) & (leave > index)
            excess = jnp.maximum(here - 1.5, 0.0)
            before = before + jnp.where(inside, excess * excess * scale, 0.0)
            left = jnp.exp2(-before)
            rise = after - prev
            rise_row = load(index, 1) - load(index, -1)
            rise_col = slopes[pl.ds(index * 16 + 8 * half, 8), :]
            facing = rise * light[0] + rise_row * light[1] + rise_col * light[2]
            square = rise * rise + rise_row * rise_row + (rise_col * rise_col + 4.0)
            lit = (passed - left) * (0.3 + jnp.abs(facing) * lax.rsqrt(square))
            white = white + lit
            tinted = [tinted[ch] + lit * jnp.tanh(here * slope[ch] + offset[ch]) for ch in range(3)]
            return before, left, here, after, white, tinted

        def chunk(tile, carry, last=False):
            for s in range(depth_sub):
                index = tile * depth_sub + s
                after = behind if last and s == depth_sub - 1 else load(index + 1)
                carry = sample(index, after, carry)
            return carry

        carry = (zero, zero + 1.0, ahead, load(0), zero, [zero] * 3)
        carry = each(tiles - 1, chunk, carry)
        _, passed, _, _, white, tinted = chunk(tiles - 1, carry, last=True)
        return [0.5 * (white + tinted[ch]) for ch in range(3)], passed

    def total(cells, join):
        cells = join(cells, turn(cells, 2 * GROUP))
        return join(cells, turn(cells, GROUP))

    def over(base, half, colour, passed, state):
        reached, layers = state
        before = jnp.where(group >= 1, turn(passed, GROUP), 1.0)
        before = before * jnp.where(group >= 1, turn(before, GROUP), 1.0)
        before = before * jnp.where(group >= 2, turn(before, 2 * GROUP), 1.0) * reached
        where = (group + base).astype(F32)
        result = []
        for place, (sums, through) in zip(target, layers):
            keep = where <= place
            sums = [sums[ch] + total(jnp.where(keep, before * colour[ch], 0.0), jnp.add) for ch in range(3)]
            through = through * total(jnp.where(keep, passed, 1.0), jnp.multiply)
            result.append((sums, through))
        return reached * total(passed, jnp.multiply), result

    def four(index, states):
        base = index * PER
        spread(base)
        end = slab_len - 1
        result = []
        for half in range(2):
            last_one, state = states[half]
            top = 8 + 8 * half
            final = cells[pl.ds(end * UNIT + top, 8), :]
            rolled = turn(final, GROUP)
            ahead = jnp.where(group == 0, last_one, rolled)
            start = turn(cells[pl.ds(top, 8), :], -GROUP)
            if isinstance(index, int) and base + PER >= slabs:
                beyond = zero
            else:
                following = jnp.minimum(base + PER, slabs - PER)
                raw = chunk_ref[following * tiles].astype(F32)[8 * half:8 * half + 8]
                beyond = jnp.where(base + PER < slabs, turn(raw, -GROUP), zero)
            behind = jnp.where(group == PER - 1, beyond, start)
            colour, passed = march(base, half, ahead, behind)
            result.append((rolled, over(base, half, colour, passed, state)))
        return result

    empty = (zero + 1.0, [([zero] * 3, zero + 1.0) for _ in range(2)])
    states = [(zero, empty) for _ in range(2)]
    if slabs == PER:
        states = four(0, states)
    else:
        states = lax.fori_loop(0, slabs // PER, four, states)
    for half in range(2):
        _, (_, layers) = states[half]
        for ref, (sums, through) in zip((mine_ref, other_ref), layers):
            ref[8 * half:8 * half + 8, :] = jnp.where(
                group == 0, sums[0], jnp.where(group == 1, sums[1], jnp.where(group == 2, sums[2], through))
            )


def join_kernel(setting_ref, mine_ref, other_ref, out_ref):
    _, group, _ = places()
    right = setting_ref[11] > 0.5
    for half in range(2):
        rows = slice(8 * half, 8 * half + 8)
        mine, other = mine_ref[rows, :], other_ref[rows, :]
        low = jnp.where(right, other, mine)
        high = jnp.where(right, mine, other)
        for ch in range(4):
            both = jnp.where(group == 0, turn(low, -GROUP * ch), turn(high, GROUP - GROUP * ch))
            out_ref[0, ch, rows, :] = both[:, :2 * GROUP]


def body(volume, ray_entry, ray_exit, palette, light_dir):
    tiles = lax.axis_size("tile")
    slabs = lax.axis_size("depth")
    depth_sub, rows_two, columns = volume.shape
    rows, col_dev = ray_entry.shape
    slab_len = depth_sub * tiles
    devices = tiles * slabs
    small = devices <= 64
    vmem = pl.BlockSpec(memory_space=VMEM)
    resident = functools.partial(pltpu.with_memory_space_constraint, memory_space=VMEM)
    where = lax.axis_index("depth").astype(jnp.int32)
    side = where % 2
    partner = where + 1 - 2 * side

    scalars = jnp.concatenate([
        palette[:, 0] * 0.5,
        palette[:, 1] * 0.5,
        light_dir * 0.7,
        jnp.stack([where, partner, side]).astype(F32),
    ])
    setting = resident(jnp.broadcast_to(scalars[:, None, None], (12, 8, LANES)))
    span = jnp.stack([ray_entry, ray_exit])
    span = jnp.where(side == 0, span[:, :, :GROUP], span[:, :, GROUP:])
    span = jnp.concatenate([span - k * slab_len for k in range(PER)], axis=2)

    chunks = pl.pallas_call(
        functools.partial(pack_kernel, slabs),
        out_shape=(pltpu.VMEM if small else jax.ShapeDtypeStruct)((devices, CHUNK, LANES), volume.dtype),
        in_specs=[vmem],
        out_specs=vmem,
        scratch_shapes=[pltpu.VMEM((columns // LANES, 128, LANES), F32)],
        name="pack",
    )(jnp.transpose(volume, (1, 0, 2)))
    chunks = lax.all_to_all(chunks, ("depth", "tile"), split_axis=0, concat_axis=0, tiled=True)
    mine, other = pl.pallas_call(
        functools.partial(ray_kernel, tiles, slabs, 64.0 / (slab_len * slabs)),
        out_shape=[pltpu.VMEM((rows, LANES), F32)] * 2,
        in_specs=[vmem] * 3,
        out_specs=[vmem] * 2,
        scratch_shapes=[pltpu.VMEM((slab_len * UNIT, LANES), F32), pltpu.VMEM((slab_len * 16, LANES), F32)],
        name="ray",
    )(setting, resident(span), resident(chunks) if small else chunks)
    other = lax.ppermute(other, "depth", [(i, i ^ 1) for i in range(slabs)])
    return pl.pallas_call(
        join_kernel,
        out_shape=jax.ShapeDtypeStruct((1, 4, rows, col_dev), F32),
        in_specs=[vmem] * 3,
        out_specs=vmem,
        name="join",
    )(setting, resident(mine), resident(other))


def solution(mesh):
    return jax.shard_map(
        body,
        mesh=mesh,
        in_specs=(P(("depth", "tile"), None, None), P(None, "tile"), P(None, "tile"), P(), P()),
        out_specs=P("depth", None, None, "tile"),
        check_vma=False,
    )
```

```python
import functools
import math

import jax
import jax.numpy as jnp
from jax import lax
from jax.experimental import pallas as pl
from jax.experimental.pallas import tpu as pltpu
from jax.sharding import PartitionSpec as P

LANES = 128
GROUP = 32
PER = LANES // GROUP
CHUNK = 24
UNIT = 32
SHORT = 8
VMEM = pltpu.VMEM
F32 = jnp.float32


def turn(cells, by):
    return pltpu.roll(cells, by % LANES, 1)


def slide(cells, by):
    return pltpu.roll(cells, by % 8, 0)


def places():
    sub = lax.broadcasted_iota(jnp.int32, (8, LANES), 0)
    lane = lax.broadcasted_iota(jnp.int32, (8, LANES), 1)
    return sub, lane // GROUP, lane % GROUP


def exchange(rows, group):
    low, even = group < 2, group % 2 == 0
    left = [jnp.where(low, rows[i], turn(rows[i + 2], 2 * GROUP)) for i in range(2)]
    right = [jnp.where(low, turn(rows[i], -2 * GROUP), rows[i + 2]) for i in range(2)]
    out = []
    for one, two in (left, right):
        out.append(jnp.where(even, one, turn(two, GROUP)))
        out.append(jnp.where(even, turn(one, -GROUP), two))
    return out


def settle(slab_len, palette_ref, light_ref, entry_ref, exit_ref, setting_ref, span_ref):
    where = lax.axis_index("depth").astype(jnp.int32)
    side = where % 2
    scalars = [palette_ref[part, ch] * 0.5 for part in range(2) for ch in range(3)]
    scalars += [light_ref[axis] * 0.7 for axis in range(3)]
    scalars += [value.astype(F32) for value in (where, where + 1 - 2 * side, side)]
    for index, value in enumerate(scalars):
        setting_ref[index] = jnp.full((8, LANES), value, F32)
    _, group, _ = places()
    right = jnp.full((8, LANES), side, jnp.int32) > 0
    for end, ref in enumerate((entry_ref, exit_ref)):
        for half in range(2):
            rows = slice(8 * half, 8 * half + 8)
            span = ref[rows, :]
            span = jnp.concatenate([span, jnp.zeros((8, LANES - span.shape[1]), jnp.int32)], axis=1)
            span = jnp.where(right, turn(span, -GROUP), span)
            span = jnp.where(group == 0, span, turn(span, GROUP))
            span = jnp.where(group < 2, span, turn(span, 2 * GROUP))
            span_ref[end, rows, :] = span - group * slab_len


def pack_kernel(
    slabs, palette_ref, light_ref, entry_ref, exit_ref, cells_ref, setting_ref, span_ref, chunk_ref, staged
):
    rows_two, depth_sub, columns = cells_ref.shape
    blocks = columns // LANES
    tiles = columns // (2 * GROUP)
    flat = rows_two * depth_sub
    settle(depth_sub * tiles, palette_ref, light_ref, entry_ref, exit_ref, setting_ref, span_ref)
    sub, group, col = places()
    lead = 7 * depth_sub
    for block in range(blocks):
        part = cells_ref[:, :, block * LANES:(block + 1) * LANES].astype(F32)
        staged[block, lead:lead + flat, :] = part.reshape(flat, LANES)

    def rows_of(block, sub_sample, row):
        return staged[block, pl.ds(lead + row * depth_sub + sub_sample, 8, stride=depth_sub), :]

    ready = {}

    def half_tile(index):
        if index < 0 or index >= blocks * PER:
            return [jnp.zeros((8, LANES), F32)] * 3
        block = index // PER
        if block not in ready:
            first = [rows_of(block, s, 1) for s in range(depth_sub)]
            second = [rows_of(block, s, 9) for s in range(depth_sub)]
            outer = [
                jnp.where(sub == 7, rows_of(block, s, -7), rows_of(block, s, rows_two - 1))
                for s in range(depth_sub)
            ]
            ready[block] = [exchange(part, group) for part in (first, second, outer)]
        return [part[index % PER] for part in ready[block]]

    for index in range(blocks * PER):
        before, here, after = (half_tile(index + step) for step in (-1, 0, 1))
        edge = [
            jnp.where(col == 0, turn(before[a], 1 - GROUP), turn(after[a], GROUP - 1))
            for a in range(2)
        ]
        second = jnp.where(col == 1, turn(edge[1], 1), turn(edge[1], -1))
        rest = jnp.where(
            sub == 1,
            slide(edge[0], 1),
            jnp.where(sub == 6, slide(edge[0], -1), jnp.where(sub == 2, slide(edge[1], 2), slide(edge[1], -2))),
        )
        rest = jnp.where(col == 2, turn(rest, 2), turn(rest, -2))
        halo = jnp.where(
            (col == 0) | (col == GROUP - 1), edge[0], jnp.where((col == 1) | (col == GROUP - 2), second, rest)
        )
        outer = jnp.where((sub == 0) | (sub == 7), here[2], halo)
        chunk = jnp.concatenate([here[0], here[1], outer], axis=0).astype(chunk_ref.dtype)
        for slab in range(index % 2, slabs, 2):
            chunk_ref[slab * tiles + index // 2] = chunk


def ray_kernel(tiles, slabs, optical_scale, setting_ref, span_ref, chunk_ref, mine_ref, other_ref, cells, slopes):
    depth_sub = PER
    slab_len = tiles * depth_sub
    slope = [setting_ref[ch] for ch in range(3)]
    offset = [setting_ref[3 + ch] for ch in range(3)]
    light = [setting_ref[6 + axis] for axis in range(3)]
    target = [setting_ref[9], setting_ref[10]]
    scale = optical_scale * math.log2(math.e)
    sub, group, col = places()
    zero = jnp.zeros((8, LANES), F32)
    unroll = tiles <= SHORT

    def each(count, step, carry):
        if unroll:
            for index in range(count):
                carry = step(index, carry)
            return carry
        return lax.fori_loop(0, count, step, carry)

    def spread(base):
        def step(tile, nothing):
            wide = [chunk_ref[(base + k) * tiles + tile].astype(F32) for k in range(PER)]
            first, second, outer = (
                exchange([part[8 * a:8 * a + 8] for part in wide], group) for a in range(3)
            )
            for s in range(depth_sub):
                at = (tile * depth_sub + s) * UNIT
                flank = outer[s]
                two = jnp.where(col == 0, turn(flank, -1), turn(flank, 1))
                rest = jnp.where(col == 0, turn(flank, -2), turn(flank, 2))
                inner = (sub > 0) & (sub < 7)
                edge = [
                    jnp.where(inner, flank, jnp.where(sub == 0, slide(rest, -1), slide(rest, 1))),
                    jnp.where(inner, two, jnp.where(sub == 0, slide(rest, -2), slide(rest, 2))),
                ]
                cells[pl.ds(at, 8), :] = flank
                cells[pl.ds(at + 24, 8), :] = flank
                for a, here in ((0, first[s]), (1, second[s])):
                    cells[pl.ds(at + 8 + 8 * a, 8), :] = here
                    rise = jnp.where(col == GROUP - 1, edge[a], turn(here, -1)) - jnp.where(
                        col == 0, edge[a], turn(here, 1)
                    )
                    slopes[pl.ds((tile * depth_sub + s) * 16 + 8 * a, 8), :] = rise
            return nothing

        each(tiles, step, 0)

    def march(base, half, ahead, behind):
        top = 8 + 8 * half
        entry = span_ref[0, 8 * half:8 * half + 8, :] - base * slab_len
        leave = span_ref[1, 8 * half:8 * half + 8, :] - base * slab_len

        def load(index, shift=0):
            return cells[pl.ds(index * UNIT + top + shift, 8), :]

        def sample(index, after, carry):
            before, passed, prev, here, white, tinted = carry
            inside = (entry <= index) & (leave > index)
            excess = jnp.maximum(here - 1.5, 0.0)
            before = before + jnp.where(inside, excess * excess * scale, 0.0)
            left = jnp.exp2(-before)
            rise = after - prev
            rise_row = load(index, 1) - load(index, -1)
            rise_col = slopes[pl.ds(index * 16 + 8 * half, 8), :]
            facing = rise * light[0] + rise_row * light[1] + rise_col * light[2]
            square = rise * rise + rise_row * rise_row + (rise_col * rise_col + 4.0)
            lit = (passed - left) * (0.3 + jnp.abs(facing) * lax.rsqrt(square))
            white = white + lit
            tinted = [tinted[ch] + lit * jnp.tanh(here * slope[ch] + offset[ch]) for ch in range(3)]
            return before, left, here, after, white, tinted

        def chunk(tile, carry, last=False):
            for s in range(depth_sub):
                index = tile * depth_sub + s
                after = behind if last and s == depth_sub - 1 else load(index + 1)
                carry = sample(index, after, carry)
            return carry

        carry = (zero, zero + 1.0, ahead, load(0), zero, [zero] * 3)
        carry = each(tiles - 1, chunk, carry)
        _, passed, _, _, white, tinted = chunk(tiles - 1, carry, last=True)
        return [0.5 * (white + tinted[ch]) for ch in range(3)], passed

    def total(cells, join):
        cells = join(cells, turn(cells, 2 * GROUP))
        return join(cells, turn(cells, GROUP))

    def over(base, half, colour, passed, state):
        reached, layers = state
        before = jnp.where(group >= 1, turn(passed, GROUP), 1.0)
        before = before * jnp.where(group >= 1, turn(before, GROUP), 1.0)
        before = before * jnp.where(group >= 2, turn(before, 2 * GROUP), 1.0) * reached
        where = (group + base).astype(F32)
        result = []
        for place, (sums, through) in zip(target, layers):
            keep = where <= place
            sums = [sums[ch] + total(jnp.where(keep, before * colour[ch], 0.0), jnp.add) for ch in range(3)]
            through = through * total(jnp.where(keep, passed, 1.0), jnp.multiply)
            result.append((sums, through))
        return reached * total(passed, jnp.multiply), result

    def four(index, states):
        base = index * PER
        spread(base)
        end = slab_len - 1
        result = []
        for half in range(2):
            last_one, state = states[half]
            top = 8 + 8 * half
            final = cells[pl.ds(end * UNIT + top, 8), :]
            rolled = turn(final, GROUP)
            ahead = jnp.where(group == 0, last_one, rolled)
            start = turn(cells[pl.ds(top, 8), :], -GROUP)
            if isinstance(index, int) and base + PER >= slabs:
                beyond = zero
            else:
                following = jnp.minimum(base + PER, slabs - PER)
                raw = chunk_ref[following * tiles].astype(F32)[8 * half:8 * half + 8]
                beyond = jnp.where(base + PER < slabs, turn(raw, -GROUP), zero)
            behind = jnp.where(group == PER - 1, beyond, start)
            colour, passed = march(base, half, ahead, behind)
            result.append((rolled, over(base, half, colour, passed, state)))
        return result

    empty = (zero + 1.0, [([zero] * 3, zero + 1.0) for _ in range(2)])
    states = [(zero, empty) for _ in range(2)]
    if slabs == PER:
        states = four(0, states)
    else:
        states = lax.fori_loop(0, slabs // PER, four, states)
    for half in range(2):
        _, (_, layers) = states[half]
        for ref, (sums, through) in zip((mine_ref, other_ref), layers):
            ref[8 * half:8 * half + 8, :] = jnp.where(
                group == 0, sums[0], jnp.where(group == 1, sums[1], jnp.where(group == 2, sums[2], through))
            )


def join_kernel(setting_ref, mine_ref, other_ref, out_ref):
    _, group, _ = places()
    right = setting_ref[11] > 0.5
    for half in range(2):
        rows = slice(8 * half, 8 * half + 8)
        mine, other = mine_ref[rows, :], other_ref[rows, :]
        low = jnp.where(right, other, mine)
        high = jnp.where(right, mine, other)
        for ch in range(4):
            both = jnp.where(group == 0, turn(low, -GROUP * ch), turn(high, GROUP - GROUP * ch))
            out_ref[0, ch, rows, :] = both[:, :2 * GROUP]


def body(volume, ray_entry, ray_exit, palette, light_dir):
    tiles = lax.axis_size("tile")
    slabs = lax.axis_size("depth")
    depth_sub, rows_two, columns = volume.shape
    rows, col_dev = ray_entry.shape
    slab_len = depth_sub * tiles
    devices = tiles * slabs
    small = devices <= 64
    vmem = pl.BlockSpec(memory_space=VMEM)
    resident = functools.partial(pltpu.with_memory_space_constraint, memory_space=VMEM)
    smem = pl.BlockSpec(memory_space=pltpu.SMEM)
    chunks_shape = (devices, CHUNK, LANES)

    setting, span, chunks = pl.pallas_call(
        functools.partial(pack_kernel, slabs),
        out_shape=[
            pltpu.VMEM((12, 8, LANES), F32),
            pltpu.VMEM((2, rows, LANES), jnp.int32),
            (pltpu.VMEM if small else jax.ShapeDtypeStruct)(chunks_shape, volume.dtype),
        ],
        in_specs=[smem] * 2 + [vmem] * 3,
        out_specs=[vmem] * 3,
        scratch_shapes=[pltpu.VMEM((columns // LANES, 128, LANES), F32)],
        name="pack",
    )(palette.T, light_dir, ray_entry, ray_exit, jnp.transpose(volume, (1, 0, 2)))
    chunks = lax.all_to_all(chunks, ("depth", "tile"), split_axis=0, concat_axis=0, tiled=True)
    mine, other = pl.pallas_call(
        functools.partial(ray_kernel, tiles, slabs, 64.0 / (slab_len * slabs)),
        out_shape=[pltpu.VMEM((rows, LANES), F32)] * 2,
        in_specs=[vmem] * 3,
        out_specs=[vmem] * 2,
        scratch_shapes=[pltpu.VMEM((slab_len * UNIT, LANES), F32), pltpu.VMEM((slab_len * 16, LANES), F32)],
        name="ray",
    )(resident(setting), resident(span), resident(chunks) if small else chunks)
    other = lax.ppermute(other, "depth", [(i, i ^ 1) for i in range(slabs)])
    return pl.pallas_call(
        join_kernel,
        out_shape=jax.ShapeDtypeStruct((1, 4, rows, col_dev), F32),
        in_specs=[vmem] * 3,
        out_specs=vmem,
        name="join",
    )(resident(setting), resident(mine), resident(other))


def solution(mesh):
    return jax.shard_map(
        body,
        mesh=mesh,
        in_specs=(P(("depth", "tile"), None, None), P(None, "tile"), P(None, "tile"), P(), P()),
        out_specs=P("depth", None, None, "tile"),
        check_vma=False,
    )
```

```python
import functools
import math

import jax
import jax.numpy as jnp
from jax import lax
from jax.experimental import pallas as pl
from jax.experimental.pallas import tpu as pltpu
from jax.sharding import PartitionSpec as P

LANES = 128
GROUP = 32
PER = LANES // GROUP
CHUNK = 20
BATCH = 8
UNIT = 32
SHORT = 8
VMEM = pltpu.VMEM
F32 = jnp.float32


def turn(cells, by):
    return pltpu.roll(cells, by % LANES, 1)


def slide(cells, by):
    return pltpu.roll(cells, by % 8, 0)


def places():
    sub = lax.broadcasted_iota(jnp.int32, (8, LANES), 0)
    lane = lax.broadcasted_iota(jnp.int32, (8, LANES), 1)
    return sub, lane // GROUP, lane % GROUP


def exchange(rows, group):
    low, even = group < 2, group % 2 == 0
    left = [jnp.where(low, rows[i], turn(rows[i + 2], 2 * GROUP)) for i in range(2)]
    right = [jnp.where(low, turn(rows[i], -2 * GROUP), rows[i + 2]) for i in range(2)]
    out = []
    for one, two in (left, right):
        out.append(jnp.where(even, one, turn(two, GROUP)))
        out.append(jnp.where(even, turn(one, -GROUP), two))
    return out


def settle(slab_len, palette_ref, light_ref, entry_ref, exit_ref, setting_ref, span_ref):
    where = lax.axis_index("depth").astype(jnp.int32)
    side = where % 2
    scalars = [palette_ref[part, ch] * 0.5 for part in range(2) for ch in range(3)]
    scalars += [light_ref[axis] * 0.7 for axis in range(3)]
    scalars += [value.astype(F32) for value in (where, where + 1 - 2 * side, side)]
    for index, value in enumerate(scalars):
        setting_ref[index] = jnp.full((8, LANES), value, F32)
    _, group, _ = places()
    right = jnp.full((8, LANES), side, jnp.int32) > 0
    for end, ref in enumerate((entry_ref, exit_ref)):
        for half in range(2):
            rows = slice(8 * half, 8 * half + 8)
            span = ref[rows, :]
            span = jnp.concatenate([span, jnp.zeros((8, LANES - span.shape[1]), jnp.int32)], axis=1)
            span = jnp.where(right, turn(span, -GROUP), span)
            span = jnp.where(group == 0, span, turn(span, GROUP))
            span = jnp.where(group < 2, span, turn(span, 2 * GROUP))
            span_ref[end, rows, :] = span - group * slab_len


def pack_kernel(
    slabs, palette_ref, light_ref, entry_ref, exit_ref, cells_ref, setting_ref, span_ref, chunk_ref, staged, flanks, ready
):
    rows_two, depth_sub, columns = cells_ref.shape
    blocks = columns // LANES
    halves = blocks * PER
    tiles = columns // (2 * GROUP)
    flat = rows_two * depth_sub
    settle(depth_sub * tiles, palette_ref, light_ref, entry_ref, exit_ref, setting_ref, span_ref)
    sub, group, _ = places()
    lead = 32
    pick = lax.broadcasted_iota(jnp.int32, (16, LANES), 0)
    lane = lax.broadcasted_iota(jnp.int32, (16, LANES), 1)
    pick = (lane == GROUP * (pick % PER) + (GROUP - 1) * (pick // PER)).astype(F32).astype(cells_ref.dtype)
    parts = []
    for block in range(blocks):
        part = cells_ref[:, :, block * LANES:(block + 1) * LANES].astype(F32)
        staged[block, lead:lead + flat, :] = part.reshape(flat, LANES)
        staged[block, lead + flat:lead + LANES, :] = jnp.zeros((LANES - flat, LANES), F32)
        whole = staged[block, lead:lead + LANES, :].astype(cells_ref.dtype)
        turned = lax.dot_general(pick, whole, (((1,), (1,)), ((), ())), preferred_element_type=F32)
        flanks[16 * block:16 * block + 16, :] = turned

    def rows_of(block, sub_sample, row):
        return staged[block, pl.ds(lead + row * depth_sub + sub_sample, 8, stride=depth_sub), :]

    def flank(index, end):
        if index < 0 or index >= halves:
            return jnp.zeros((8, LANES), F32)
        at = 16 * (index // PER) + index % PER + PER * end
        return jnp.broadcast_to(flanks[pl.ds(at, 1), :], (8, LANES))

    for block in range(blocks):
        first = exchange([rows_of(block, s, 1) for s in range(depth_sub)], group)
        second = exchange([rows_of(block, s, 9) for s in range(depth_sub)], group)
        outer = exchange(
            [jnp.where(sub == 3, rows_of(block, s, -3), rows_of(block, s, rows_two - 1)) for s in range(depth_sub)],
            group,
        )
        for place in range(PER):
            index = block * PER + place
            tail = jnp.where(
                sub == 1, flank(index - 1, 1), jnp.where(sub == 2, flank(index + 1, 0), outer[place])
            )
            at = 24 * index
            ready[at:at + 8, :] = first[place]
            ready[at + 8:at + 16, :] = second[place]
            ready[at + 16:at + 24, :] = tail
            for piece in range(CHUNK // 4):
                rows = ready[at + 4 * piece:at + 4 * piece + 4, :].astype(chunk_ref.dtype)
                for slab in range(index % 2, slabs, 2):
                    chunk_ref[slab * tiles + index // 2, piece] = rows


def ray_kernel(tiles, slabs, optical_scale, setting_ref, span_ref, chunk_ref, mine_ref, other_ref, cells, slopes, wide, sides, edges):
    depth_sub = PER
    slab_len = tiles * depth_sub
    slope = [setting_ref[ch] for ch in range(3)]
    offset = [setting_ref[3 + ch] for ch in range(3)]
    light = [setting_ref[6 + axis] for axis in range(3)]
    target = [setting_ref[9], setting_ref[10]]
    scale = optical_scale * math.log2(math.e)
    sub, group, col = places()
    zero = jnp.zeros((8, LANES), F32)
    unroll = tiles <= SHORT

    def each(count, step, carry):
        if unroll:
            for index in range(count):
                carry = step(index, carry)
            return carry
        return lax.fori_loop(0, count, step, carry)

    eye = lax.broadcasted_iota(jnp.int32, (80, LANES), 0) == lax.broadcasted_iota(jnp.int32, (80, LANES), 1)
    eye = eye.astype(F32).astype(chunk_ref.dtype)
    source = lax.broadcasted_iota(jnp.int32, (LANES, LANES), 0)
    drain = lax.broadcasted_iota(jnp.int32, (LANES, LANES), 1)
    same = source // GROUP == drain // GROUP
    band = jnp.where(same & (source == drain + 1), 1.0, 0.0) - jnp.where(same & (source == drain - 1), 1.0, 0.0)
    band = band.astype(chunk_ref.dtype)
    odd = (sub % 2 == 1, (sub % 2 == 1) & (sub < 7))

    def unpack(base):
        count = PER * tiles * CHUNK
        start = base * tiles * CHUNK
        step = 160

        def piece(index, nothing):
            at = index * step
            if not (isinstance(at, int) and isinstance(start, int)):
                at = pl.multiple_of(at, 32)
            wide[pl.ds(at, step), :] = chunk_ref[pl.ds(pl.multiple_of(start + at, 32), step), :].astype(F32)
            return nothing

        each(count // step, piece, 0)

    def line_up(batch):
        for k in range(PER):
            for end in range(2):
                at = (k * tiles + batch * BATCH) * CHUNK + 17 + end
                sides[pl.ds(k * GROUP + (GROUP - 1) * end, BATCH, stride=2), :] = wide[pl.ds(at, BATCH, stride=CHUNK), :]
        for part in range(2):
            rows = slice(8 * part, 8 * part + 8)
            sides[rows, :] = jnp.where(odd[part], sides[LANES + 8 * part:LANES + 8 * part + 8, :], sides[rows, :])
        edges[...] = lax.dot_general(
            eye, sides[0:LANES, :].astype(chunk_ref.dtype), (((1,), (1,)), ((), ())), preferred_element_type=F32
        )

    def put(tile, slot):
        first, second, outer = (
            exchange([wide[pl.ds((k * tiles + tile) * CHUNK + at, 8), :] for k in range(PER)], group)
            for at in (0, 8, 12)
        )
        stack = jnp.concatenate(first + second, axis=0).astype(chunk_ref.dtype)
        inner = jnp.dot(stack, band, preferred_element_type=F32)
        for s in range(depth_sub):
            at = (tile * depth_sub + s) * UNIT
            cells[pl.ds(at, 8), :] = outer[s]
            cells[pl.ds(at + 20, 8), :] = outer[s]
            for a, here in ((0, first[s]), (1, second[s])):
                cells[pl.ds(at + 8 + 8 * a, 8), :] = here
                edge = edges[pl.ds((1 + 8 * a) * depth_sub + s, 8, stride=depth_sub), :]
                edge = turn(edge, -2 * slot) if slot else edge
                row = 8 * (PER * a + s)
                rise = inner[row:row + 8] + jnp.where(col == 0, -edge, jnp.where(col == GROUP - 1, edge, 0.0))
                slopes[pl.ds((tile * depth_sub + s) * 16 + 8 * a, 8), :] = rise

    def march(base, aheads, behinds, feed):
        tops = (8, 16)
        entry = [span_ref[0, 8 * half:8 * half + 8, :] - base * slab_len for half in range(2)]
        leave = [span_ref[1, 8 * half:8 * half + 8, :] - base * slab_len for half in range(2)]

        def load(half, index, shift=0):
            return cells[pl.ds(index * UNIT + tops[half] + shift, 8), :]

        def sample(half, index, after, carry):
            before, passed, prev, here, white, tinted = carry
            inside = (entry[half] <= index) & (leave[half] > index)
            excess = jnp.maximum(here - 1.5, 0.0)
            before = before + jnp.where(inside, excess * excess * scale, 0.0)
            left = jnp.exp2(-before)
            rise = after - prev
            rise_row = load(half, index, 1) - load(half, index, -1)
            rise_col = slopes[pl.ds(index * 16 + 8 * half, 8), :]
            facing = rise * light[0] + rise_row * light[1] + rise_col * light[2]
            square = rise * rise + rise_row * rise_row + (rise_col * rise_col + 4.0)
            lit = (passed - left) * (0.3 + jnp.abs(facing) * lax.rsqrt(square))
            white = white + lit
            tinted = [tinted[ch] + lit * jnp.tanh(here * slope[ch] + offset[ch]) for ch in range(3)]
            return before, left, here, after, white, tinted

        def chunk(tile, carries, last=False):
            if not last:
                feed(tile + 1)
            carries = list(carries)
            for s in range(depth_sub):
                index = tile * depth_sub + s
                for half in range(2):
                    final = last and s == depth_sub - 1
                    after = behinds[half] if final else load(half, index + 1)
                    carries[half] = sample(half, index, after, carries[half])
            return carries

        carries = [
            (zero, zero + 1.0, aheads[half], load(half, 0), zero, [zero] * 3) for half in range(2)
        ]
        carries = each(tiles - 1, chunk, carries)
        carries = chunk(tiles - 1, carries, last=True)
        return [
            ([0.5 * (carry[4] + carry[5][ch]) for ch in range(3)], carry[1]) for carry in carries
        ]

    def total(cells, join):
        cells = join(cells, turn(cells, 2 * GROUP))
        return join(cells, turn(cells, GROUP))

    def over(base, half, colour, passed, state):
        reached, layers = state
        before = jnp.where(group >= 1, turn(passed, GROUP), 1.0)
        before = before * jnp.where(group >= 1, turn(before, GROUP), 1.0)
        before = before * jnp.where(group >= 2, turn(before, 2 * GROUP), 1.0) * reached
        where = (group + base).astype(F32)
        result = []
        for place, (sums, through) in zip(target, layers):
            keep = where <= place
            sums = [sums[ch] + total(jnp.where(keep, before * colour[ch], 0.0), jnp.add) for ch in range(3)]
            through = through * total(jnp.where(keep, passed, 1.0), jnp.multiply)
            result.append((sums, through))
        return reached * total(passed, jnp.multiply), result

    def four(index, states):
        base = index * PER
        end = slab_len - 1
        unpack(base)
        if unroll:
            line_up(0)
            put(tiles - 1, tiles - 1)
            put(0, 0)
        else:

            def batch(number, nothing):
                line_up(number)
                for slot in range(BATCH):
                    put(number * BATCH + slot, slot)
                return nothing

            lax.fori_loop(0, tiles // BATCH, batch, 0)
        rolled, aheads, behinds = [], [], []
        for half in range(2):
            top = 8 + 8 * half
            rolled.append(turn(cells[pl.ds(end * UNIT + top, 8), :], GROUP))
            aheads.append(jnp.where(group == 0, states[half][0], rolled[half]))
            start = turn(cells[pl.ds(top, 8), :], -GROUP)
            if isinstance(index, int) and base + PER >= slabs:
                beyond = zero
            else:
                following = jnp.minimum(base + PER, slabs - PER)
                at = pl.multiple_of(following * (tiles * CHUNK), 32)
                raw = chunk_ref[pl.ds(at, 16), :].astype(F32)[8 * half:8 * half + 8]
                beyond = jnp.where(base + PER < slabs, turn(raw, -GROUP), zero)
            behinds.append(jnp.where(group == PER - 1, beyond, start))

        def feed(tile):
            if unroll and tile < tiles - 1:
                put(tile, tile)

        found = march(base, aheads, behinds, feed)
        return [
            (rolled[half], over(base, half, *found[half], states[half][1])) for half in range(2)
        ]

    empty = (zero + 1.0, [([zero] * 3, zero + 1.0) for _ in range(2)])
    states = [(zero, empty) for _ in range(2)]
    if slabs == PER:
        states = four(0, states)
    else:
        states = lax.fori_loop(0, slabs // PER, four, states)
    for half in range(2):
        _, (_, layers) = states[half]
        for ref, (sums, through) in zip((mine_ref, other_ref), layers):
            ref[8 * half:8 * half + 8, :] = jnp.where(
                group == 0, sums[0], jnp.where(group == 1, sums[1], jnp.where(group == 2, sums[2], through))
            )


def join_kernel(setting_ref, mine_ref, other_ref, out_ref):
    _, group, _ = places()
    right = setting_ref[11] > 0.5
    for half in range(2):
        rows = slice(8 * half, 8 * half + 8)
        mine, other = mine_ref[rows, :], other_ref[rows, :]
        low = jnp.where(right, other, mine)
        high = jnp.where(right, mine, other)
        for ch in range(4):
            both = jnp.where(group == 0, turn(low, -GROUP * ch), turn(high, GROUP - GROUP * ch))
            out_ref[0, ch, rows, :] = both[:, :2 * GROUP]


def body(volume, ray_entry, ray_exit, palette, light_dir):
    tiles = lax.axis_size("tile")
    slabs = lax.axis_size("depth")
    depth_sub, rows_two, columns = volume.shape
    rows, col_dev = ray_entry.shape
    slab_len = depth_sub * tiles
    devices = tiles * slabs
    small = devices <= 64
    vmem = pl.BlockSpec(memory_space=VMEM)
    resident = functools.partial(pltpu.with_memory_space_constraint, memory_space=VMEM)
    smem = pl.BlockSpec(memory_space=pltpu.SMEM)
    chunks_shape = (devices, CHUNK // 4, 4, LANES)

    setting, span, chunks = pl.pallas_call(
        functools.partial(pack_kernel, slabs),
        out_shape=[
            pltpu.VMEM((12, 8, LANES), F32),
            pltpu.VMEM((2, rows, LANES), jnp.int32),
            (pltpu.VMEM if small else jax.ShapeDtypeStruct)(chunks_shape, volume.dtype),
        ],
        in_specs=[smem] * 2 + [vmem] * 3,
        out_specs=[vmem] * 3,
        scratch_shapes=[
            pltpu.VMEM((columns // LANES, 160, LANES), F32),
            pltpu.VMEM((16 * (columns // LANES), LANES), F32),
            pltpu.VMEM((24 * (columns // GROUP), LANES), F32),
        ],
        name="pack",
    )(palette.T, light_dir, ray_entry, ray_exit, jnp.transpose(volume, (1, 0, 2)))
    chunks = lax.all_to_all(chunks, ("depth", "tile"), split_axis=0, concat_axis=0, tiled=True)
    chunks = chunks.reshape(devices * CHUNK, LANES)
    mine, other = pl.pallas_call(
        functools.partial(ray_kernel, tiles, slabs, 64.0 / (slab_len * slabs)),
        out_shape=[pltpu.VMEM((rows, LANES), F32)] * 2,
        in_specs=[vmem] * 3,
        out_specs=[vmem] * 2,
        scratch_shapes=[
            pltpu.VMEM((slab_len * UNIT, LANES), F32),
            pltpu.VMEM((slab_len * 16, LANES), F32),
            pltpu.VMEM((PER * tiles * CHUNK, LANES), F32),
            pltpu.VMEM((LANES + 16, LANES), F32),
            pltpu.VMEM((80, LANES), F32),
        ],
        name="ray",
    )(resident(setting), resident(span), resident(chunks) if small else chunks)
    other = lax.ppermute(other, "depth", [(i, i ^ 1) for i in range(slabs)])
    return pl.pallas_call(
        join_kernel,
        out_shape=jax.ShapeDtypeStruct((1, 4, rows, col_dev), F32),
        in_specs=[vmem] * 3,
        out_specs=vmem,
        name="join",
    )(resident(setting), resident(mine), resident(other))


def solution(mesh):
    return jax.shard_map(
        body,
        mesh=mesh,
        in_specs=(P(("depth", "tile"), None, None), P(None, "tile"), P(None, "tile"), P(), P()),
        out_specs=P("depth", None, None, "tile"),
        check_vma=False,
    )
```

```python
import functools
import math

import jax
import jax.numpy as jnp
from jax import lax
from jax.experimental import pallas as pl
from jax.experimental.pallas import tpu as pltpu
from jax.sharding import PartitionSpec as P

LANES = 128
GROUP = 32
PER = LANES // GROUP
CHUNK = 20
BATCH = 8
UNIT = 32
SHORT = 8
VMEM = pltpu.VMEM
F32 = jnp.float32


def turn(cells, by):
    return pltpu.roll(cells, by % LANES, 1)


def slide(cells, by):
    return pltpu.roll(cells, by % 8, 0)


def places():
    sub = lax.broadcasted_iota(jnp.int32, (8, LANES), 0)
    lane = lax.broadcasted_iota(jnp.int32, (8, LANES), 1)
    return sub, lane // GROUP, lane % GROUP


def exchange(rows, group):
    out = []
    for to in range(PER):
        moved = [turn(row, GROUP * (of - to)) if of != to else row for of, row in enumerate(rows)]
        out.append(
            jnp.where(group < 2, jnp.where(group == 0, moved[0], moved[1]), jnp.where(group == 2, moved[2], moved[3]))
        )
    return out


def settle(slab_len, palette_ref, light_ref, entry_ref, exit_ref, setting_ref, span_ref):
    where = lax.axis_index("depth").astype(jnp.int32)
    side = where % 2
    scalars = [palette_ref[part, ch] * 0.5 for part in range(2) for ch in range(3)]
    scalars += [light_ref[axis] * 0.7 for axis in range(3)]
    scalars += [value.astype(F32) for value in (where, where + 1 - 2 * side, side)]
    for index, value in enumerate(scalars):
        setting_ref[index] = jnp.full((8, LANES), value, F32)
    _, group, _ = places()
    right = jnp.full((8, LANES), side, jnp.int32) > 0
    for end, ref in enumerate((entry_ref, exit_ref)):
        for half in range(2):
            rows = slice(8 * half, 8 * half + 8)
            span = ref[rows, :]
            span = jnp.concatenate([span, jnp.zeros((8, LANES - span.shape[1]), jnp.int32)], axis=1)
            span = jnp.where(right, turn(span, -GROUP), span)
            span = jnp.where(group == 0, span, turn(span, GROUP))
            span = jnp.where(group < 2, span, turn(span, 2 * GROUP))
            span_ref[end, rows, :] = span - group * slab_len


def pack_kernel(
    slabs, palette_ref, light_ref, entry_ref, exit_ref, cells_ref, setting_ref, span_ref, chunk_ref, staged, flanks, ready
):
    rows_two, depth_sub, columns = cells_ref.shape
    blocks = columns // LANES
    halves = blocks * PER
    tiles = columns // (2 * GROUP)
    flat = rows_two * depth_sub
    settle(depth_sub * tiles, palette_ref, light_ref, entry_ref, exit_ref, setting_ref, span_ref)
    sub, group, _ = places()
    lead = 32
    pick = lax.broadcasted_iota(jnp.int32, (16, LANES), 0)
    lane = lax.broadcasted_iota(jnp.int32, (16, LANES), 1)
    hit = lane == GROUP * (pick % PER) + (GROUP - 1) * (pick // PER)
    pick = jnp.where(hit, jnp.where(pick // PER == 1, -1.0, 1.0), 0.0).astype(cells_ref.dtype)
    for block in range(blocks):
        part = cells_ref[:, :, block * LANES:(block + 1) * LANES].astype(F32)
        staged[block, lead:lead + flat, :] = part.reshape(flat, LANES)
        staged[block, lead + flat:lead + LANES, :] = jnp.zeros((LANES - flat, LANES), F32)
        whole = staged[block, lead:lead + LANES, :].astype(cells_ref.dtype)
        turned = lax.dot_general(pick, whole, (((1,), (1,)), ((), ())), preferred_element_type=F32)
        flanks[16 * block:16 * block + 16, :] = turned

    def rows_of(block, sub_sample, row):
        return staged[block, pl.ds(lead + row * depth_sub + sub_sample, 8, stride=depth_sub), :]

    def flank(index, end):
        if index < 0 or index >= halves:
            return jnp.zeros((8, LANES), F32)
        at = 16 * (index // PER) + index % PER + PER * end
        return jnp.broadcast_to(flanks[pl.ds(at, 1), :], (8, LANES))

    for block in range(blocks):
        first = exchange([rows_of(block, s, 1) for s in range(depth_sub)], group)
        second = exchange([rows_of(block, s, 9) for s in range(depth_sub)], group)
        outer = exchange(
            [jnp.where(sub == 3, rows_of(block, s, -3), rows_of(block, s, rows_two - 1)) for s in range(depth_sub)],
            group,
        )
        for place in range(PER):
            index = block * PER + place
            tail = jnp.where(
                sub == 1, flank(index - 1, 1), jnp.where(sub == 2, flank(index + 1, 0), outer[place])
            )
            at = 24 * index
            ready[at:at + 8, :] = first[place]
            ready[at + 8:at + 16, :] = second[place]
            ready[at + 16:at + 24, :] = tail
            for piece in range(CHUNK // 4):
                rows = ready[at + 4 * piece:at + 4 * piece + 4, :].astype(chunk_ref.dtype)
                for slab in range(index % 2, slabs, 2):
                    chunk_ref[slab * tiles + index // 2, piece] = rows


def ray_kernel(tiles, slabs, optical_scale, setting_ref, span_ref, chunk_ref, mine_ref, other_ref, cells, slopes, wide, sides, edges):
    depth_sub = PER
    slab_len = tiles * depth_sub
    slope = [setting_ref[ch] for ch in range(3)]
    offset = [setting_ref[3 + ch] for ch in range(3)]
    light = [setting_ref[6 + axis] for axis in range(3)]
    target = [setting_ref[9], setting_ref[10]]
    scale = optical_scale * math.log2(math.e)
    sub, group, col = places()
    zero = jnp.zeros((8, LANES), F32)
    unroll = tiles <= SHORT

    def each(count, step, carry):
        if unroll:
            for index in range(count):
                carry = step(index, carry)
            return carry
        return lax.fori_loop(0, count, step, carry)

    eye = lax.broadcasted_iota(jnp.int32, (80, LANES), 0) == lax.broadcasted_iota(jnp.int32, (80, LANES), 1)
    eye = eye.astype(F32).astype(chunk_ref.dtype)
    source = lax.broadcasted_iota(jnp.int32, (LANES, LANES), 0)
    drain = lax.broadcasted_iota(jnp.int32, (LANES, LANES), 1)
    same = source // GROUP == drain // GROUP
    band = jnp.where(same & (source == drain + 1), 1.0, 0.0) - jnp.where(same & (source == drain - 1), 1.0, 0.0)
    band = band.astype(chunk_ref.dtype)
    odd = (sub % 2 == 1, (sub % 2 == 1) & (sub < 7))
    rim = (col == 0) | (col == GROUP - 1)

    def unpack(base):
        count = PER * tiles * CHUNK
        start = base * tiles * CHUNK
        step = 160

        def piece(index, nothing):
            at = index * step
            if not (isinstance(at, int) and isinstance(start, int)):
                at = pl.multiple_of(at, 32)
            wide[pl.ds(at, step), :] = chunk_ref[pl.ds(pl.multiple_of(start + at, 32), step), :].astype(F32)
            return nothing

        each(count // step, piece, 0)

    def line_up(batch):
        for k in range(PER):
            for end in range(2):
                at = (k * tiles + batch * BATCH) * CHUNK + 17 + end
                sides[pl.ds(k * GROUP + (GROUP - 1) * end, BATCH, stride=2), :] = wide[pl.ds(at, BATCH, stride=CHUNK), :]
        for part in range(2):
            rows = slice(8 * part, 8 * part + 8)
            sides[rows, :] = jnp.where(odd[part], sides[LANES + 8 * part:LANES + 8 * part + 8, :], sides[rows, :])
        edges[...] = lax.dot_general(
            eye, sides[0:LANES, :].astype(chunk_ref.dtype), (((1,), (1,)), ((), ())), preferred_element_type=F32
        )

    def put(tile, slot):
        first, second, outer = (
            exchange([wide[pl.ds((k * tiles + tile) * CHUNK + at, 8), :] for k in range(PER)], group)
            for at in (0, 8, 12)
        )
        stack = jnp.concatenate(first + second, axis=0).astype(chunk_ref.dtype)
        inner = jnp.dot(stack, band, preferred_element_type=F32)
        for s in range(depth_sub):
            at = (tile * depth_sub + s) * UNIT
            cells[pl.ds(at, 8), :] = outer[s]
            cells[pl.ds(at + 20, 8), :] = outer[s]
            for a, here in ((0, first[s]), (1, second[s])):
                cells[pl.ds(at + 8 + 8 * a, 8), :] = here
                edge = edges[pl.ds((1 + 8 * a) * depth_sub + s, 8, stride=depth_sub), :]
                edge = turn(edge, -2 * slot) if slot else edge
                row = 8 * (PER * a + s)
                rise = inner[row:row + 8] + jnp.where(rim, edge, 0.0)
                slopes[pl.ds((tile * depth_sub + s) * 16 + 8 * a, 8), :] = rise

    def march(base, aheads, behinds, feed):
        tops = (8, 16)
        entry = [span_ref[0, 8 * half:8 * half + 8, :] - base * slab_len for half in range(2)]
        leave = [span_ref[1, 8 * half:8 * half + 8, :] - base * slab_len for half in range(2)]

        def load(half, index, shift=0):
            return cells[pl.ds(index * UNIT + tops[half] + shift, 8), :]

        def sample(half, index, after, carry):
            before, passed, prev, here, white, tinted = carry
            inside = (entry[half] <= index) & (leave[half] > index)
            excess = jnp.maximum(here - 1.5, 0.0)
            before = before - jnp.where(inside, excess * excess * scale, 0.0)
            left = jnp.exp2(before)
            rise = after - prev
            rise_row = load(half, index, 1) - load(half, index, -1)
            rise_col = slopes[pl.ds(index * 16 + 8 * half, 8), :]
            facing = rise * light[0] + rise_row * light[1] + rise_col * light[2]
            square = rise * rise + rise_row * rise_row + (rise_col * rise_col + 4.0)
            lit = (passed - left) * (0.3 + jnp.abs(facing) * lax.rsqrt(square))
            white = white + lit
            tinted = [tinted[ch] + lit * jnp.tanh(here * slope[ch] + offset[ch]) for ch in range(3)]
            return before, left, here, after, white, tinted

        def chunk(tile, carries, last=False):
            if not last:
                feed(tile + 1)
            carries = list(carries)
            for s in range(depth_sub):
                index = tile * depth_sub + s
                for half in range(2):
                    final = last and s == depth_sub - 1
                    after = behinds[half] if final else load(half, index + 1)
                    carries[half] = sample(half, index, after, carries[half])
            return carries

        carries = [
            (zero, zero + 1.0, aheads[half], load(half, 0), zero, [zero] * 3) for half in range(2)
        ]
        carries = each(tiles - 1, chunk, carries)
        carries = chunk(tiles - 1, carries, last=True)
        return [
            ([0.5 * (carry[4] + carry[5][ch]) for ch in range(3)], carry[1]) for carry in carries
        ]

    def total(cells, join):
        return join(join(cells, turn(cells, GROUP)), join(turn(cells, 2 * GROUP), turn(cells, 3 * GROUP)))

    def over(base, half, colour, passed, state):
        reached, layers = state
        before = reached
        for step in range(1, PER):
            before = before * jnp.where(group >= step, turn(passed, step * GROUP), 1.0)
        where = (group + base).astype(F32)
        result = []
        for place, (sums, through) in zip(target, layers):
            keep = where <= place
            sums = [sums[ch] + total(jnp.where(keep, before * colour[ch], 0.0), jnp.add) for ch in range(3)]
            through = through * total(jnp.where(keep, passed, 1.0), jnp.multiply)
            result.append((sums, through))
        return reached * total(passed, jnp.multiply), result

    def four(index, states):
        base = index * PER
        end = slab_len - 1
        unpack(base)
        if unroll:
            line_up(0)
            put(tiles - 1, tiles - 1)
            put(0, 0)
        else:

            def batch(number, nothing):
                line_up(number)
                for slot in range(BATCH):
                    put(number * BATCH + slot, slot)
                return nothing

            lax.fori_loop(0, tiles // BATCH, batch, 0)
        rolled, aheads, behinds = [], [], []
        for half in range(2):
            top = 8 + 8 * half
            rolled.append(turn(cells[pl.ds(end * UNIT + top, 8), :], GROUP))
            aheads.append(jnp.where(group == 0, states[half][0], rolled[half]))
            start = turn(cells[pl.ds(top, 8), :], -GROUP)
            if isinstance(index, int) and base + PER >= slabs:
                beyond = zero
            else:
                following = jnp.minimum(base + PER, slabs - PER)
                at = pl.multiple_of(following * (tiles * CHUNK), 32)
                raw = chunk_ref[pl.ds(at, 16), :].astype(F32)[8 * half:8 * half + 8]
                beyond = jnp.where(base + PER < slabs, turn(raw, -GROUP), zero)
            behinds.append(jnp.where(group == PER - 1, beyond, start))

        def feed(tile):
            if unroll and tile < tiles - 1:
                put(tile, tile)

        found = march(base, aheads, behinds, feed)
        return [
            (rolled[half], over(base, half, *found[half], states[half][1])) for half in range(2)
        ]

    empty = (zero + 1.0, [([zero] * 3, zero + 1.0) for _ in range(2)])
    states = [(zero, empty) for _ in range(2)]
    if slabs == PER:
        states = four(0, states)
    else:
        states = lax.fori_loop(0, slabs // PER, four, states)
    for half in range(2):
        _, (_, layers) = states[half]
        for ref, (sums, through) in zip((mine_ref, other_ref), layers):
            for ch, value in enumerate((*sums, through)):
                ref[ch, 8 * half:8 * half + 8, :] = value


def join_kernel(setting_ref, mine_ref, other_ref, out_ref):
    _, group, _ = places()
    own = (group == 1) == (setting_ref[11] > 0.5)
    for half in range(2):
        rows = slice(8 * half, 8 * half + 8)
        for ch in range(4):
            both = jnp.where(own, mine_ref[ch, rows, :], other_ref[ch, rows, :])
            out_ref[0, ch, rows, :] = both[:, :2 * GROUP]


def body(volume, ray_entry, ray_exit, palette, light_dir):
    tiles = lax.axis_size("tile")
    slabs = lax.axis_size("depth")
    depth_sub, rows_two, columns = volume.shape
    rows, col_dev = ray_entry.shape
    slab_len = depth_sub * tiles
    devices = tiles * slabs
    small = devices <= 64
    vmem = pl.BlockSpec(memory_space=VMEM)
    resident = functools.partial(pltpu.with_memory_space_constraint, memory_space=VMEM)
    smem = pl.BlockSpec(memory_space=pltpu.SMEM)
    chunks_shape = (devices, CHUNK // 4, 4, LANES)

    setting, span, chunks = pl.pallas_call(
        functools.partial(pack_kernel, slabs),
        out_shape=[
            pltpu.VMEM((12, 8, LANES), F32),
            pltpu.VMEM((2, rows, LANES), jnp.int32),
            (pltpu.VMEM if small else jax.ShapeDtypeStruct)(chunks_shape, volume.dtype),
        ],
        in_specs=[smem] * 2 + [vmem] * 3,
        out_specs=[vmem] * 3,
        scratch_shapes=[
            pltpu.VMEM((columns // LANES, 160, LANES), F32),
            pltpu.VMEM((16 * (columns // LANES), LANES), F32),
            pltpu.VMEM((24 * (columns // GROUP), LANES), F32),
        ],
        name="pack",
    )(palette.T, light_dir, ray_entry, ray_exit, jnp.transpose(volume, (1, 0, 2)))
    chunks = lax.all_to_all(chunks, ("depth", "tile"), split_axis=0, concat_axis=0, tiled=True)
    chunks = chunks.reshape(devices * CHUNK, LANES)
    mine, other = pl.pallas_call(
        functools.partial(ray_kernel, tiles, slabs, 64.0 / (slab_len * slabs)),
        out_shape=[pltpu.VMEM((4, rows, LANES), F32)] * 2,
        in_specs=[vmem] * 3,
        out_specs=[vmem] * 2,
        scratch_shapes=[
            pltpu.VMEM((slab_len * UNIT, LANES), F32),
            pltpu.VMEM((slab_len * 16, LANES), F32),
            pltpu.VMEM((PER * tiles * CHUNK + 32, LANES), F32),
            pltpu.VMEM((LANES + 16, LANES), F32),
            pltpu.VMEM((80, LANES), F32),
        ],
        name="ray",
    )(resident(setting), resident(span), resident(chunks) if small else chunks)
    other = lax.ppermute(other, "depth", [(i, i ^ 1) for i in range(slabs)])
    return pl.pallas_call(
        join_kernel,
        out_shape=jax.ShapeDtypeStruct((1, 4, rows, col_dev), F32),
        in_specs=[vmem] * 3,
        out_specs=vmem,
        name="join",
    )(resident(setting), resident(mine), resident(other))


def solution(mesh):
    return jax.shard_map(
        body,
        mesh=mesh,
        in_specs=(P(("depth", "tile"), None, None), P(None, "tile"), P(None, "tile"), P(), P()),
        out_specs=P("depth", None, None, "tile"),
        check_vma=False,
    )
```

```python
import functools
import math

import jax
import jax.numpy as jnp
from jax import lax
from jax.experimental import pallas as pl
from jax.experimental.pallas import tpu as pltpu
from jax.sharding import PartitionSpec as P

LANES = 128
GROUP = 32
PER = LANES // GROUP
CHUNK = 20
BATCH = 8
PIECES = 3
UNIT = 32
SHORT = 8
VMEM = pltpu.VMEM
F32 = jnp.float32


def turn(cells, by):
    return pltpu.roll(cells, by % LANES, 1)


def slide(cells, by):
    return pltpu.roll(cells, by % 8, 0)


def places():
    sub = lax.broadcasted_iota(jnp.int32, (8, LANES), 0)
    lane = lax.broadcasted_iota(jnp.int32, (8, LANES), 1)
    return sub, lane // GROUP, lane % GROUP


def exchange(rows, group):
    out = []
    for to in range(PER):
        moved = [turn(row, GROUP * (of - to)) if of != to else row for of, row in enumerate(rows)]
        out.append(
            jnp.where(group < 2, jnp.where(group == 0, moved[0], moved[1]), jnp.where(group == 2, moved[2], moved[3]))
        )
    return out


def settle(slab_len, palette_ref, light_ref, entry_ref, exit_ref, setting_ref, span_ref):
    where = lax.axis_index("depth").astype(jnp.int32)
    side = where % 2
    scalars = [palette_ref[part, ch] * 0.5 for part in range(2) for ch in range(3)]
    scalars += [light_ref[axis] * 0.7 for axis in range(3)]
    scalars += [value.astype(F32) for value in (where, where + 1 - 2 * side, side)]
    for index, value in enumerate(scalars):
        setting_ref[index] = jnp.full((8, LANES), value, F32)
    _, group, _ = places()
    right = jnp.full((8, LANES), side, jnp.int32) > 0
    for end, ref in enumerate((entry_ref, exit_ref)):
        for half in range(2):
            rows = slice(8 * half, 8 * half + 8)
            span = ref[rows, :]
            span = jnp.concatenate([span, jnp.zeros((8, LANES - span.shape[1]), jnp.int32)], axis=1)
            span = jnp.where(right, turn(span, -GROUP), span)
            span = jnp.where(group == 0, span, turn(span, GROUP))
            span = jnp.where(group < 2, span, turn(span, 2 * GROUP))
            span_ref[end, rows, :] = span - group * slab_len


def pack_kernel(slabs, *refs):
    pieces = refs[:PIECES]
    palette_ref, light_ref, entry_ref, exit_ref, setting_ref, span_ref, chunk_ref, staged, flanks, ready = refs[PIECES:]
    rows_piece, depth_sub, columns = pieces[0].shape
    rows_two = PIECES * rows_piece
    blocks = columns // LANES
    halves = blocks * PER
    tiles = columns // (2 * GROUP)
    flat = rows_two * depth_sub
    settle(depth_sub * tiles, palette_ref, light_ref, entry_ref, exit_ref, setting_ref, span_ref)
    sub, group, _ = places()
    lead = 32
    pick = lax.broadcasted_iota(jnp.int32, (16, LANES), 0)
    lane = lax.broadcasted_iota(jnp.int32, (16, LANES), 1)
    hit = lane == GROUP * (pick % PER) + (GROUP - 1) * (pick // PER)
    pick = jnp.where(hit, jnp.where(pick // PER == 1, -1.0, 1.0), 0.0).astype(chunk_ref.dtype)
    for block in range(blocks):
        for number, piece_ref in enumerate(pieces):
            part = piece_ref[:, :, block * LANES:(block + 1) * LANES].astype(F32)
            size = rows_piece * depth_sub
            staged[block, lead + number * size:lead + (number + 1) * size, :] = part.reshape(size, LANES)
        staged[block, lead + flat:lead + LANES, :] = jnp.zeros((LANES - flat, LANES), F32)
        whole = staged[block, lead:lead + LANES, :].astype(chunk_ref.dtype)
        turned = lax.dot_general(pick, whole, (((1,), (1,)), ((), ())), preferred_element_type=F32)
        flanks[16 * block:16 * block + 16, :] = turned

    def rows_of(block, sub_sample, row):
        return staged[block, pl.ds(lead + row * depth_sub + sub_sample, 8, stride=depth_sub), :]

    def flank(index, end):
        if index < 0 or index >= halves:
            return jnp.zeros((8, LANES), F32)
        at = 16 * (index // PER) + index % PER + PER * end
        return jnp.broadcast_to(flanks[pl.ds(at, 1), :], (8, LANES))

    for block in range(blocks):
        first = exchange([rows_of(block, s, 1) for s in range(depth_sub)], group)
        second = exchange([rows_of(block, s, 9) for s in range(depth_sub)], group)
        outer = exchange(
            [jnp.where(sub == 3, rows_of(block, s, -3), rows_of(block, s, rows_two - 1)) for s in range(depth_sub)],
            group,
        )
        for place in range(PER):
            index = block * PER + place
            tail = jnp.where(
                sub == 1, flank(index - 1, 1), jnp.where(sub == 2, flank(index + 1, 0), outer[place])
            )
            side, at = index % 2, CHUNK * (index // 2)
            ready[side, at:at + 8, :] = first[place]
            ready[side, at + 8:at + 16, :] = second[place]
            ready[side, at + 16:at + 20, :] = tail[:4]
    for side in range(2):
        for at in range(0, tiles * CHUNK, 32):
            rows = ready[side, at:at + 32, :].astype(chunk_ref.dtype)
            for slab in range(side, slabs, 2):
                start = slab * tiles * CHUNK + at
                chunk_ref[start:start + 32, :] = rows


def ray_kernel(tiles, slabs, optical_scale, setting_ref, span_ref, chunk_ref, mine_ref, other_ref, cells, slopes, wide, sides, edges):
    depth_sub = PER
    slab_len = tiles * depth_sub
    slope = [setting_ref[ch] for ch in range(3)]
    offset = [setting_ref[3 + ch] for ch in range(3)]
    light = [setting_ref[6 + axis] for axis in range(3)]
    target = [setting_ref[9], setting_ref[10]]
    scale = optical_scale * math.log2(math.e)
    sub, group, col = places()
    zero = jnp.zeros((8, LANES), F32)
    unroll = tiles <= SHORT

    def each(count, step, carry):
        if unroll:
            for index in range(count):
                carry = step(index, carry)
            return carry
        return lax.fori_loop(0, count, step, carry)

    eye = lax.broadcasted_iota(jnp.int32, (80, LANES), 0) == lax.broadcasted_iota(jnp.int32, (80, LANES), 1)
    eye = eye.astype(F32).astype(chunk_ref.dtype)
    source = lax.broadcasted_iota(jnp.int32, (LANES, LANES), 0)
    drain = lax.broadcasted_iota(jnp.int32, (LANES, LANES), 1)
    same = source // GROUP == drain // GROUP
    band = jnp.where(same & (source == drain + 1), 1.0, 0.0) - jnp.where(same & (source == drain - 1), 1.0, 0.0)
    band = band.astype(chunk_ref.dtype)
    odd = (sub % 2 == 1, (sub % 2 == 1) & (sub < 7))
    rim = (col == 0) | (col == GROUP - 1)

    def unpack(base):
        count = PER * tiles * CHUNK
        start = base * tiles * CHUNK
        step = 160

        def piece(index, nothing):
            at = index * step
            if not (isinstance(at, int) and isinstance(start, int)):
                at = pl.multiple_of(at, 32)
            wide[pl.ds(at, step), :] = chunk_ref[pl.ds(pl.multiple_of(start + at, 32), step), :].astype(F32)
            return nothing

        each(count // step, piece, 0)

    def line_up(batch):
        for k in range(PER):
            for end in range(2):
                at = (k * tiles + batch * BATCH) * CHUNK + 17 + end
                sides[pl.ds(k * GROUP + (GROUP - 1) * end, BATCH, stride=2), :] = wide[pl.ds(at, BATCH, stride=CHUNK), :]
        for part in range(2):
            rows = slice(8 * part, 8 * part + 8)
            sides[rows, :] = jnp.where(odd[part], sides[LANES + 8 * part:LANES + 8 * part + 8, :], sides[rows, :])
        edges[...] = lax.dot_general(
            eye, sides[0:LANES, :].astype(chunk_ref.dtype), (((1,), (1,)), ((), ())), preferred_element_type=F32
        )

    def put(tile, slot):
        first, second, outer = (
            exchange([wide[pl.ds((k * tiles + tile) * CHUNK + at, 8), :] for k in range(PER)], group)
            for at in (0, 8, 12)
        )
        stack = jnp.concatenate(first + second, axis=0).astype(chunk_ref.dtype)
        inner = jnp.dot(stack, band, preferred_element_type=F32)
        for s in range(depth_sub):
            at = (tile * depth_sub + s) * UNIT
            cells[pl.ds(at, 8), :] = outer[s]
            cells[pl.ds(at + 20, 8), :] = outer[s]
            for a, here in ((0, first[s]), (1, second[s])):
                cells[pl.ds(at + 8 + 8 * a, 8), :] = here
                edge = edges[pl.ds((1 + 8 * a) * depth_sub + s, 8, stride=depth_sub), :]
                edge = turn(edge, -2 * slot) if slot else edge
                row = 8 * (PER * a + s)
                rise = inner[row:row + 8] + jnp.where(rim, edge, 0.0)
                slopes[pl.ds((tile * depth_sub + s) * 16 + 8 * a, 8), :] = rise

    def march(base, aheads, behinds, feed):
        tops = (8, 16)
        entry = [span_ref[0, 8 * half:8 * half + 8, :] - base * slab_len for half in range(2)]
        leave = [span_ref[1, 8 * half:8 * half + 8, :] - base * slab_len for half in range(2)]

        def load(half, index, shift=0):
            return cells[pl.ds(index * UNIT + tops[half] + shift, 8), :]

        def sample(half, index, after, carry):
            before, passed, prev, here, white, tinted = carry
            inside = (entry[half] <= index) & (leave[half] > index)
            excess = jnp.maximum(here - 1.5, 0.0)
            before = before - jnp.where(inside, excess * excess * scale, 0.0)
            left = jnp.exp2(before)
            rise = after - prev
            rise_row = load(half, index, 1) - load(half, index, -1)
            rise_col = slopes[pl.ds(index * 16 + 8 * half, 8), :]
            facing = rise * light[0] + rise_row * light[1] + rise_col * light[2]
            square = rise * rise + rise_row * rise_row + (rise_col * rise_col + 4.0)
            lit = (passed - left) * (0.3 + jnp.abs(facing) * lax.rsqrt(square))
            white = white + lit
            tinted = [tinted[ch] + lit * jnp.tanh(here * slope[ch] + offset[ch]) for ch in range(3)]
            return before, left, here, after, white, tinted

        def chunk(tile, carries, last=False):
            if not last:
                feed(tile + 1)
            carries = list(carries)
            for s in range(depth_sub):
                index = tile * depth_sub + s
                for half in range(2):
                    final = last and s == depth_sub - 1
                    after = behinds[half] if final else load(half, index + 1)
                    carries[half] = sample(half, index, after, carries[half])
            return carries

        carries = [
            (zero, zero + 1.0, aheads[half], load(half, 0), zero, [zero] * 3) for half in range(2)
        ]
        carries = each(tiles - 1, chunk, carries)
        carries = chunk(tiles - 1, carries, last=True)
        return [
            ([0.5 * (carry[4] + carry[5][ch]) for ch in range(3)], carry[1]) for carry in carries
        ]

    def total(cells, join):
        return join(join(cells, turn(cells, GROUP)), join(turn(cells, 2 * GROUP), turn(cells, 3 * GROUP)))

    def over(base, half, colour, passed, state):
        reached, layers = state
        before = reached
        for step in range(1, PER):
            before = before * jnp.where(group >= step, turn(passed, step * GROUP), 1.0)
        where = (group + base).astype(F32)
        result = []
        for place, (sums, through) in zip(target, layers):
            keep = where <= place
            sums = [sums[ch] + total(jnp.where(keep, before * colour[ch], 0.0), jnp.add) for ch in range(3)]
            through = through * total(jnp.where(keep, passed, 1.0), jnp.multiply)
            result.append((sums, through))
        return reached * total(passed, jnp.multiply), result

    def four(index, states):
        base = index * PER
        end = slab_len - 1
        unpack(base)
        if unroll:
            line_up(0)
            put(tiles - 1, tiles - 1)
            put(0, 0)
        else:

            def batch(number, nothing):
                line_up(number)
                for slot in range(BATCH):
                    put(number * BATCH + slot, slot)
                return nothing

            lax.fori_loop(0, tiles // BATCH, batch, 0)
        rolled, aheads, behinds = [], [], []
        for half in range(2):
            top = 8 + 8 * half
            rolled.append(turn(cells[pl.ds(end * UNIT + top, 8), :], GROUP))
            aheads.append(jnp.where(group == 0, states[half][0], rolled[half]))
            start = turn(cells[pl.ds(top, 8), :], -GROUP)
            if isinstance(index, int) and base + PER >= slabs:
                beyond = zero
            else:
                following = jnp.minimum(base + PER, slabs - PER)
                at = pl.multiple_of(following * (tiles * CHUNK), 32)
                raw = chunk_ref[pl.ds(at, 16), :].astype(F32)[8 * half:8 * half + 8]
                beyond = jnp.where(base + PER < slabs, turn(raw, -GROUP), zero)
            behinds.append(jnp.where(group == PER - 1, beyond, start))

        def feed(tile):
            if unroll and tile < tiles - 1:
                put(tile, tile)

        found = march(base, aheads, behinds, feed)
        return [
            (rolled[half], over(base, half, *found[half], states[half][1])) for half in range(2)
        ]

    empty = (zero + 1.0, [([zero] * 3, zero + 1.0) for _ in range(2)])
    states = [(zero, empty) for _ in range(2)]
    if slabs == PER:
        states = four(0, states)
    else:
        states = lax.fori_loop(0, slabs // PER, four, states)
    for half in range(2):
        _, (_, layers) = states[half]
        for ref, (sums, through) in zip((mine_ref, other_ref), layers):
            for ch, value in enumerate((*sums, through)):
                ref[ch, 8 * half:8 * half + 8, :] = value


def join_kernel(setting_ref, mine_ref, other_ref, out_ref):
    _, group, _ = places()
    own = (group == 1) == (setting_ref[11] > 0.5)
    for half in range(2):
        rows = slice(8 * half, 8 * half + 8)
        for ch in range(4):
            both = jnp.where(own, mine_ref[ch, rows, :], other_ref[ch, rows, :])
            out_ref[0, ch, rows, :] = both[:, :2 * GROUP]


def body(volume, ray_entry, ray_exit, palette, light_dir):
    tiles = lax.axis_size("tile")
    slabs = lax.axis_size("depth")
    depth_sub, rows_two, columns = volume.shape
    rows, col_dev = ray_entry.shape
    slab_len = depth_sub * tiles
    devices = tiles * slabs
    small = devices <= 64
    vmem = pl.BlockSpec(memory_space=VMEM)
    resident = functools.partial(pltpu.with_memory_space_constraint, memory_space=VMEM)
    smem = pl.BlockSpec(memory_space=pltpu.SMEM)
    chunks_shape = (devices * CHUNK, LANES)

    cells = jnp.transpose(volume, (1, 0, 2))
    shape = (rows_two // PIECES, depth_sub, columns)
    windows = [pl.BlockSpec(shape, functools.partial(lambda piece, _: (piece, 0, 0), piece)) for piece in range(PIECES)]
    setting, span, chunks = pl.pallas_call(
        functools.partial(pack_kernel, slabs),
        out_shape=[
            pltpu.VMEM((12, 8, LANES), F32),
            pltpu.VMEM((2, rows, LANES), jnp.int32),
            (pltpu.VMEM if small else jax.ShapeDtypeStruct)(chunks_shape, volume.dtype),
        ],
        grid=(1,),
        in_specs=windows + [smem] * 2 + [vmem] * 2,
        out_specs=[vmem] * 3,
        scratch_shapes=[
            pltpu.VMEM((columns // LANES, 160, LANES), F32),
            pltpu.VMEM((16 * (columns // LANES), LANES), F32),
            pltpu.VMEM((2, tiles * CHUNK, LANES), F32),
        ],
        name="pack",
    )(*[cells] * PIECES, palette.T, light_dir, ray_entry, ray_exit)
    chunks = chunks.reshape(devices, CHUNK // 4, 4, LANES)
    chunks = lax.all_to_all(chunks, ("depth", "tile"), split_axis=0, concat_axis=0, tiled=True)
    chunks = chunks.reshape(devices * CHUNK, LANES)
    mine, other = pl.pallas_call(
        functools.partial(ray_kernel, tiles, slabs, 64.0 / (slab_len * slabs)),
        out_shape=[pltpu.VMEM((4, rows, LANES), F32)] * 2,
        in_specs=[vmem] * 3,
        out_specs=[vmem] * 2,
        scratch_shapes=[
            pltpu.VMEM((slab_len * UNIT, LANES), F32),
            pltpu.VMEM((slab_len * 16, LANES), F32),
            pltpu.VMEM((PER * tiles * CHUNK + 32, LANES), F32),
            pltpu.VMEM((LANES + 16, LANES), F32),
            pltpu.VMEM((80, LANES), F32),
        ],
        name="ray",
    )(resident(setting), resident(span), resident(chunks) if small else chunks)
    other = lax.ppermute(other, "depth", [(i, i ^ 1) for i in range(slabs)])
    return pl.pallas_call(
        join_kernel,
        out_shape=jax.ShapeDtypeStruct((1, 4, rows, col_dev), F32),
        in_specs=[vmem] * 3,
        out_specs=vmem,
        name="join",
    )(resident(setting), resident(mine), resident(other))


def solution(mesh):
    return jax.shard_map(
        body,
        mesh=mesh,
        in_specs=(P(("depth", "tile"), None, None), P(None, "tile"), P(None, "tile"), P(), P()),
        out_specs=P("depth", None, None, "tile"),
        check_vma=False,
    )
```

```python
import functools
import math

import jax
import jax.numpy as jnp
from jax import lax
from jax.experimental import pallas as pl
from jax.experimental.pallas import tpu as pltpu
from jax.sharding import PartitionSpec as P

LANES = 128
GROUP = 32
PER = LANES // GROUP
CHUNK = 20
BATCH = 8
PIECES = 3
UNIT = 32
SHORT = 8
VMEM = pltpu.VMEM
F32 = jnp.float32


def turn(cells, by):
    return pltpu.roll(cells, by % LANES, 1)


def slide(cells, by):
    return pltpu.roll(cells, by % 8, 0)


def places():
    sub = lax.broadcasted_iota(jnp.int32, (8, LANES), 0)
    lane = lax.broadcasted_iota(jnp.int32, (8, LANES), 1)
    return sub, lane // GROUP, lane % GROUP


def exchange(rows, group):
    out = []
    for to in range(PER):
        moved = [turn(row, GROUP * (of - to)) if of != to else row for of, row in enumerate(rows)]
        out.append(
            jnp.where(group < 2, jnp.where(group == 0, moved[0], moved[1]), jnp.where(group == 2, moved[2], moved[3]))
        )
    return out


def settle(slab_len, palette_ref, light_ref, entry_ref, exit_ref, setting_ref, span_ref):
    where = lax.axis_index("depth").astype(jnp.int32)
    side = where % 2
    scalars = [palette_ref[part, ch] * 0.5 for part in range(2) for ch in range(3)]
    scalars += [light_ref[axis] * 0.7 for axis in range(3)]
    scalars += [value.astype(F32) for value in (where, where + 1 - 2 * side, side)]
    for index, value in enumerate(scalars):
        setting_ref[index] = jnp.full((8, LANES), value, F32)
    _, group, _ = places()
    right = jnp.full((8, LANES), side, jnp.int32) > 0
    for end, ref in enumerate((entry_ref, exit_ref)):
        for half in range(2):
            rows = slice(8 * half, 8 * half + 8)
            span = ref[rows, :]
            span = jnp.concatenate([span, jnp.zeros((8, LANES - span.shape[1]), jnp.int32)], axis=1)
            span = jnp.where(right, turn(span, -GROUP), span)
            span = jnp.where(group == 0, span, turn(span, GROUP))
            span = jnp.where(group < 2, span, turn(span, 2 * GROUP))
            span_ref[end, rows, :] = span - group * slab_len


def pack_kernel(slabs, *refs):
    pieces = refs[:PIECES]
    palette_ref, light_ref, entry_ref, exit_ref, setting_ref, span_ref, chunk_ref, staged, flanks, ready = refs[PIECES:]
    rows_piece, depth_sub, columns = pieces[0].shape
    rows_two = PIECES * rows_piece
    blocks = columns // LANES
    halves = blocks * PER
    tiles = columns // (2 * GROUP)
    flat = rows_two * depth_sub
    settle(depth_sub * tiles, palette_ref, light_ref, entry_ref, exit_ref, setting_ref, span_ref)
    sub, group, _ = places()
    lead = 32
    pick = lax.broadcasted_iota(jnp.int32, (16, LANES), 0)
    lane = lax.broadcasted_iota(jnp.int32, (16, LANES), 1)
    hit = lane == GROUP * (pick % PER) + (GROUP - 1) * (pick // PER)
    pick = jnp.where(hit, jnp.where(pick // PER == 1, -1.0, 1.0), 0.0).astype(chunk_ref.dtype)
    for block in range(blocks):
        for number, piece_ref in enumerate(pieces):
            part = piece_ref[:, :, block * LANES:(block + 1) * LANES].astype(F32)
            size = rows_piece * depth_sub
            staged[block, lead + number * size:lead + (number + 1) * size, :] = part.reshape(size, LANES)
        staged[block, lead + flat:lead + LANES, :] = jnp.zeros((LANES - flat, LANES), F32)
        whole = staged[block, lead:lead + LANES, :].astype(chunk_ref.dtype)
        turned = lax.dot_general(pick, whole, (((1,), (1,)), ((), ())), preferred_element_type=F32)
        flanks[16 * block:16 * block + 16, :] = turned

    def rows_of(block, sub_sample, row):
        return staged[block, pl.ds(lead + row * depth_sub + sub_sample, 8, stride=depth_sub), :]

    def flank(index, end):
        if index < 0 or index >= halves:
            return jnp.zeros((8, LANES), F32)
        at = 16 * (index // PER) + index % PER + PER * end
        return jnp.broadcast_to(flanks[pl.ds(at, 1), :], (8, LANES))

    for block in range(blocks):
        first = exchange([rows_of(block, s, 1) for s in range(depth_sub)], group)
        second = exchange([rows_of(block, s, 9) for s in range(depth_sub)], group)
        outer = exchange(
            [jnp.where(sub == 3, rows_of(block, s, -3), rows_of(block, s, rows_two - 1)) for s in range(depth_sub)],
            group,
        )
        for place in range(PER):
            index = block * PER + place
            tail = jnp.where(
                sub == 1, flank(index - 1, 1), jnp.where(sub == 2, flank(index + 1, 0), outer[place])
            )
            side, at = index % 2, CHUNK * (index // 2)
            ready[side, at:at + 8, :] = first[place]
            ready[side, at + 8:at + 16, :] = second[place]
            ready[side, at + 16:at + 20, :] = tail[:4]
    for side in range(2):
        for at in range(0, tiles * CHUNK, 32):
            rows = ready[side, at:at + 32, :].astype(chunk_ref.dtype)
            for slab in range(side, slabs, 2):
                start = slab * tiles * CHUNK + at
                chunk_ref[start:start + 32, :] = rows


def ray_kernel(tiles, slabs, optical_scale, setting_ref, span_ref, chunk_ref, mine_ref, other_ref, cells, slopes, wide, sides, edges):
    depth_sub = PER
    slab_len = tiles * depth_sub
    slope = [setting_ref[ch] for ch in range(3)]
    offset = [setting_ref[3 + ch] for ch in range(3)]
    light = [setting_ref[6 + axis] for axis in range(3)]
    target = [setting_ref[9], setting_ref[10]]
    scale = optical_scale * math.log2(math.e)
    sub, group, col = places()
    zero = jnp.zeros((8, LANES), F32)
    unroll = tiles <= SHORT

    def each(count, step, carry):
        if unroll:
            for index in range(count):
                carry = step(index, carry)
            return carry
        return lax.fori_loop(0, count, step, carry)

    eye = lax.broadcasted_iota(jnp.int32, (80, LANES), 0) == lax.broadcasted_iota(jnp.int32, (80, LANES), 1)
    eye = eye.astype(F32).astype(chunk_ref.dtype)
    source = lax.broadcasted_iota(jnp.int32, (LANES, LANES), 0)
    drain = lax.broadcasted_iota(jnp.int32, (LANES, LANES), 1)
    same = source // GROUP == drain // GROUP
    band = jnp.where(same & (source == drain + 1), 1.0, 0.0) - jnp.where(same & (source == drain - 1), 1.0, 0.0)
    band = band.astype(chunk_ref.dtype)
    odd = (sub % 2 == 1, (sub % 2 == 1) & (sub < 7))
    rim = (col == 0) | (col == GROUP - 1)

    def unpack(base):
        count = PER * tiles * CHUNK
        start = base * tiles * CHUNK
        step = 160

        def piece(index, nothing):
            at = index * step
            if not (isinstance(at, int) and isinstance(start, int)):
                at = pl.multiple_of(at, 32)
            wide[pl.ds(at, step), :] = chunk_ref[pl.ds(pl.multiple_of(start + at, 32), step), :].astype(F32)
            return nothing

        each(count // step, piece, 0)

    def line_up(batch):
        for k in range(PER):
            for end in range(2):
                at = (k * tiles + batch * BATCH) * CHUNK + 17 + end
                sides[pl.ds(k * GROUP + (GROUP - 1) * end, BATCH, stride=2), :] = wide[pl.ds(at, BATCH, stride=CHUNK), :]
        for part in range(2):
            rows = slice(8 * part, 8 * part + 8)
            sides[rows, :] = jnp.where(odd[part], sides[LANES + 8 * part:LANES + 8 * part + 8, :], sides[rows, :])
        edges[...] = lax.dot_general(
            eye, sides[0:LANES, :].astype(chunk_ref.dtype), (((1,), (1,)), ((), ())), preferred_element_type=F32
        )

    def put(tile, slot):
        first, second, outer = (
            exchange([wide[pl.ds((k * tiles + tile) * CHUNK + at, 8), :] for k in range(PER)], group)
            for at in (0, 8, 12)
        )
        stack = jnp.concatenate(first + second, axis=0).astype(chunk_ref.dtype)
        inner = jnp.dot(stack, band, preferred_element_type=F32)
        for s in range(depth_sub):
            at = (tile * depth_sub + s) * UNIT
            cells[pl.ds(at, 8), :] = outer[s]
            cells[pl.ds(at + 20, 8), :] = outer[s]
            for a, here in ((0, first[s]), (1, second[s])):
                cells[pl.ds(at + 8 + 8 * a, 8), :] = here
                edge = edges[pl.ds((1 + 8 * a) * depth_sub + s, 8, stride=depth_sub), :]
                edge = turn(edge, -2 * slot) if slot else edge
                row = 8 * (PER * a + s)
                rise = inner[row:row + 8] + jnp.where(rim, edge, 0.0)
                slopes[pl.ds((tile * depth_sub + s) * 16 + 8 * a, 8), :] = rise

    def march(base, aheads, behinds, feed):
        tops = (8, 16)
        entry = [span_ref[0, 8 * half:8 * half + 8, :] - base * slab_len for half in range(2)]
        leave = [span_ref[1, 8 * half:8 * half + 8, :] - base * slab_len for half in range(2)]

        def load(half, index, shift=0):
            return cells[pl.ds(index * UNIT + tops[half] + shift, 8), :]

        def sample(half, index, after, carry):
            before, passed, prev, here, white, tinted = carry
            inside = (entry[half] <= index) & (leave[half] > index)
            excess = jnp.maximum(here - 1.5, 0.0)
            before = before - jnp.where(inside, excess * excess * scale, 0.0)
            left = jnp.exp2(before)
            rise = after - prev
            rise_row = load(half, index, 1) - load(half, index, -1)
            rise_col = slopes[pl.ds(index * 16 + 8 * half, 8), :]
            facing = rise * light[0] + rise_row * light[1] + rise_col * light[2]
            square = rise * rise + rise_row * rise_row + (rise_col * rise_col + 4.0)
            lit = (passed - left) * (0.3 + jnp.abs(facing) * lax.rsqrt(square))
            white = white + lit
            tinted = [tinted[ch] + lit * jnp.tanh(here * slope[ch] + offset[ch]) for ch in range(3)]
            return before, left, here, after, white, tinted

        def chunk(tile, carries, last=False):
            if not last:
                feed(tile + 1)
            carries = list(carries)
            for s in range(depth_sub):
                index = tile * depth_sub + s
                for half in range(2):
                    final = last and s == depth_sub - 1
                    after = behinds[half] if final else load(half, index + 1)
                    carries[half] = sample(half, index, after, carries[half])
            return carries

        carries = [
            (zero, zero + 1.0, aheads[half], load(half, 0), zero, [zero] * 3) for half in range(2)
        ]
        carries = each(tiles - 1, chunk, carries)
        carries = chunk(tiles - 1, carries, last=True)
        return [
            ([0.5 * (carry[4] + carry[5][ch]) for ch in range(3)], carry[1]) for carry in carries
        ]

    def total(cells, join):
        return join(join(cells, turn(cells, GROUP)), join(turn(cells, 2 * GROUP), turn(cells, 3 * GROUP)))

    def over(base, half, colour, passed, state):
        reached, layers = state
        before = reached
        for step in range(1, PER):
            before = before * jnp.where(group >= step, turn(passed, step * GROUP), 1.0)
        where = (group + base).astype(F32)
        result = []
        for place, (sums, through) in zip(target, layers):
            keep = where <= place
            sums = [sums[ch] + total(jnp.where(keep, before * colour[ch], 0.0), jnp.add) for ch in range(3)]
            through = through * total(jnp.where(keep, passed, 1.0), jnp.multiply)
            result.append((sums, through))
        return reached * total(passed, jnp.multiply), result

    def four(index, states):
        base = index * PER
        end = slab_len - 1
        unpack(base)
        if unroll:
            line_up(0)
            put(tiles - 1, tiles - 1)
            put(0, 0)
        else:

            def batch(number, nothing):
                line_up(number)
                for slot in range(BATCH):
                    put(number * BATCH + slot, slot)
                return nothing

            lax.fori_loop(0, tiles // BATCH, batch, 0)
        rolled, aheads, behinds = [], [], []
        for half in range(2):
            top = 8 + 8 * half
            rolled.append(turn(cells[pl.ds(end * UNIT + top, 8), :], GROUP))
            aheads.append(jnp.where(group == 0, states[half][0], rolled[half]))
            start = turn(cells[pl.ds(top, 8), :], -GROUP)
            if isinstance(index, int) and base + PER >= slabs:
                beyond = zero
            else:
                following = jnp.minimum(base + PER, slabs - PER)
                at = pl.multiple_of(following * (tiles * CHUNK), 32)
                raw = chunk_ref[pl.ds(at, 16), :].astype(F32)[8 * half:8 * half + 8]
                beyond = jnp.where(base + PER < slabs, turn(raw, -GROUP), zero)
            behinds.append(jnp.where(group == PER - 1, beyond, start))

        def feed(tile):
            if unroll and tile < tiles - 1:
                put(tile, tile)

        found = march(base, aheads, behinds, feed)
        return [
            (rolled[half], over(base, half, *found[half], states[half][1])) for half in range(2)
        ]

    def deep():
        empty = (zero + 1.0, [([zero] * 3, zero + 1.0) for _ in range(2)])
        states = [(zero, empty) for _ in range(2)]
        if slabs == PER:
            states = four(0, states)
        else:
            states = lax.fori_loop(0, slabs // PER, four, states)
        for half in range(2):
            _, (_, layers) = states[half]
            for ref, (sums, through) in zip((mine_ref, other_ref), layers):
                for ch, value in enumerate((*sums, through)):
                    ref[ch, 8 * half:8 * half + 8, :] = value

    def shallow():
        unpack(0)
        line_up(0)
        end = slab_len - 1

        def place(tile):
            def swap(at):
                return exchange(
                    [wide[pl.ds((k * tiles + tile) * CHUNK + at[a], 8), :] for a in range(2) for k in range(2)], group
                )

            centre, below, above = swap((0, 8)), swap((1, 9)), swap((12, 0))
            stack = jnp.concatenate(centre, axis=0).astype(chunk_ref.dtype)
            inner = jnp.dot(stack, band, preferred_element_type=F32)
            for s in range(depth_sub):
                at = (tile * depth_sub + s) * UNIT
                cells[pl.ds(at, 8), :] = above[s]
                cells[pl.ds(at + 9, 8), :] = below[s]
                cells[pl.ds(at + 8, 8), :] = centre[s]
                edge = [edges[pl.ds((1 + 8 * a) * depth_sub + s, 8, stride=depth_sub), :] for a in range(2)]
                edge = jnp.where(group < 2, turn(edge[0], -2 * tile), turn(edge[1], 2 * GROUP - 2 * tile))
                rise = inner[8 * s:8 * s + 8] + jnp.where(rim, edge, 0.0)
                slopes[pl.ds((tile * depth_sub + s) * 16, 8), :] = rise

        for tile in range(tiles):
            place(tile)

        def load(index, shift=0):
            return cells[pl.ds(index * UNIT + 8 + shift, 8), :]

        def span(which):
            return jnp.where(group < 2, span_ref[which, 0:8, :], turn(span_ref[which, 8:16, :], 2 * GROUP))

        entry, leave = span(0), span(1)
        odd_group = group % 2 == 1
        beyond = [wide[pl.ds(2 * tiles * CHUNK + 8 * a, 8), :] for a in range(2)]
        beyond = jnp.where(group < 2, turn(beyond[0], GROUP), turn(beyond[1], 3 * GROUP))
        behind = jnp.where(odd_group, beyond, turn(load(0), -GROUP))
        prev = jnp.where(odd_group, turn(load(end), GROUP), 0.0)
        here, before, passed, white, tinted = load(0), zero, zero + 1.0, zero, [zero] * 3
        for index in range(slab_len):
            after = behind if index == end else load(index + 1)
            inside = (entry <= index) & (leave > index)
            excess = jnp.maximum(here - 1.5, 0.0)
            before = before - jnp.where(inside, excess * excess * scale, 0.0)
            left = jnp.exp2(before)
            rise = after - prev
            rise_row = load(index, 1) - load(index, -1)
            rise_col = slopes[pl.ds(index * 16, 8), :]
            facing = rise * light[0] + rise_row * light[1] + rise_col * light[2]
            square = rise * rise + rise_row * rise_row + (rise_col * rise_col + 4.0)
            lit = (passed - left) * (0.3 + jnp.abs(facing) * lax.rsqrt(square))
            white = white + lit
            tinted = [tinted[ch] + lit * jnp.tanh(here * slope[ch] + offset[ch]) for ch in range(3)]
            passed, prev, here = left, here, after
        reached = jnp.where(odd_group, turn(passed, GROUP), 1.0)
        where = (group % 2).astype(F32)
        for goal, ref in zip(target, (mine_ref, other_ref)):
            keep = where <= goal
            parts = [jnp.where(keep, reached * (0.5 * (white + tinted[ch])), 0.0) for ch in range(3)]
            for ch, value in enumerate((*parts, jnp.where(keep, passed, 1.0))):
                join = jnp.multiply if ch == 3 else jnp.add
                value = join(value, jnp.where(odd_group, turn(value, GROUP), turn(value, -GROUP)))
                ref[ch, 0:8, :] = value
                ref[ch, 8:16, :] = turn(value, 2 * GROUP)

    if slabs == PER and unroll:
        near = lax.axis_index("depth") < 2
        pl.when(near)(shallow)
        pl.when(jnp.logical_not(near))(deep)
    else:
        deep()


def join_kernel(setting_ref, mine_ref, other_ref, out_ref):
    _, group, _ = places()
    own = (group == 1) == (setting_ref[11] > 0.5)
    for half in range(2):
        rows = slice(8 * half, 8 * half + 8)
        for ch in range(4):
            both = jnp.where(own, mine_ref[ch, rows, :], other_ref[ch, rows, :])
            out_ref[0, ch, rows, :] = both[:, :2 * GROUP]


def body(volume, ray_entry, ray_exit, palette, light_dir):
    tiles = lax.axis_size("tile")
    slabs = lax.axis_size("depth")
    depth_sub, rows_two, columns = volume.shape
    rows, col_dev = ray_entry.shape
    slab_len = depth_sub * tiles
    devices = tiles * slabs
    small = devices <= 64
    vmem = pl.BlockSpec(memory_space=VMEM)
    resident = functools.partial(pltpu.with_memory_space_constraint, memory_space=VMEM)
    smem = pl.BlockSpec(memory_space=pltpu.SMEM)
    chunks_shape = (devices * CHUNK, LANES)

    cells = jnp.transpose(volume, (1, 0, 2))
    shape = (rows_two // PIECES, depth_sub, columns)
    windows = [pl.BlockSpec(shape, functools.partial(lambda piece, _: (piece, 0, 0), piece)) for piece in range(PIECES)]
    setting, span, chunks = pl.pallas_call(
        functools.partial(pack_kernel, slabs),
        out_shape=[
            pltpu.VMEM((12, 8, LANES), F32),
            pltpu.VMEM((2, rows, LANES), jnp.int32),
            (pltpu.VMEM if small else jax.ShapeDtypeStruct)(chunks_shape, volume.dtype),
        ],
        grid=(1,),
        in_specs=windows + [smem] * 2 + [vmem] * 2,
        out_specs=[vmem] * 3,
        scratch_shapes=[
            pltpu.VMEM((columns // LANES, 160, LANES), F32),
            pltpu.VMEM((16 * (columns // LANES), LANES), F32),
            pltpu.VMEM((2, tiles * CHUNK, LANES), F32),
        ],
        name="pack",
    )(*[cells] * PIECES, palette.T, light_dir, ray_entry, ray_exit)
    chunks = chunks.reshape(devices, CHUNK // 4, 4, LANES)
    chunks = lax.all_to_all(chunks, ("depth", "tile"), split_axis=0, concat_axis=0, tiled=True)
    chunks = chunks.reshape(devices * CHUNK, LANES)
    mine, other = pl.pallas_call(
        functools.partial(ray_kernel, tiles, slabs, 64.0 / (slab_len * slabs)),
        out_shape=[pltpu.VMEM((4, rows, LANES), F32)] * 2,
        in_specs=[vmem] * 3,
        out_specs=[vmem] * 2,
        scratch_shapes=[
            pltpu.VMEM((slab_len * UNIT, LANES), F32),
            pltpu.VMEM((slab_len * 16, LANES), F32),
            pltpu.VMEM((PER * tiles * CHUNK + 32, LANES), F32),
            pltpu.VMEM((LANES + 16, LANES), F32),
            pltpu.VMEM((80, LANES), F32),
        ],
        name="ray",
    )(resident(setting), resident(span), resident(chunks) if small else chunks)
    other = lax.ppermute(other, "depth", [(i, i ^ 1) for i in range(slabs)])
    return pl.pallas_call(
        join_kernel,
        out_shape=jax.ShapeDtypeStruct((1, 4, rows, col_dev), F32),
        in_specs=[vmem] * 3,
        out_specs=vmem,
        name="join",
    )(resident(setting), resident(mine), resident(other))


def solution(mesh):
    return jax.shard_map(
        body,
        mesh=mesh,
        in_specs=(P(("depth", "tile"), None, None), P(None, "tile"), P(None, "tile"), P(), P()),
        out_specs=P("depth", None, None, "tile"),
        check_vma=False,
    )
```

```python
import functools
import math

import jax
import jax.numpy as jnp
from jax import lax
from jax.experimental import pallas as pl
from jax.experimental.pallas import tpu as pltpu
from jax.sharding import PartitionSpec as P

LANES = 128
GROUP = 32
PER = LANES // GROUP
CHUNK = 20
BATCH = 8
PIECES = 3
UNIT = 32
SHORT = 8
VMEM = pltpu.VMEM
F32 = jnp.float32


def turn(cells, by):
    return pltpu.roll(cells, by % LANES, 1)


def slide(cells, by):
    return pltpu.roll(cells, by % 8, 0)


def places():
    sub = lax.broadcasted_iota(jnp.int32, (8, LANES), 0)
    lane = lax.broadcasted_iota(jnp.int32, (8, LANES), 1)
    return sub, lane // GROUP, lane % GROUP


def exchange(rows, group):
    out = []
    for to in range(PER):
        moved = [turn(row, GROUP * (of - to)) if of != to else row for of, row in enumerate(rows)]
        out.append(
            jnp.where(group < 2, jnp.where(group == 0, moved[0], moved[1]), jnp.where(group == 2, moved[2], moved[3]))
        )
    return out


def settle(slab_len, palette_ref, light_ref, entry_ref, exit_ref, setting_ref, span_ref):
    where = lax.axis_index("depth").astype(jnp.int32)
    side = where % 2
    scalars = [palette_ref[part, ch] * 0.5 for part in range(2) for ch in range(3)]
    scalars += [light_ref[axis] * 0.7 for axis in range(3)]
    scalars += [value.astype(F32) for value in (where, where + 1 - 2 * side, side)]
    for index, value in enumerate(scalars):
        setting_ref[index] = jnp.full((8, LANES), value, F32)
    _, group, _ = places()
    right = jnp.full((8, LANES), side, jnp.int32) > 0
    for end, ref in enumerate((entry_ref, exit_ref)):
        for half in range(2):
            rows = slice(8 * half, 8 * half + 8)
            span = ref[rows, :]
            span = jnp.concatenate([span, jnp.zeros((8, LANES - span.shape[1]), jnp.int32)], axis=1)
            span = jnp.where(right, turn(span, -GROUP), span)
            span = jnp.where(group == 0, span, turn(span, GROUP))
            span = jnp.where(group < 2, span, turn(span, 2 * GROUP))
            span_ref[end, rows, :] = span - group * slab_len


def pack_kernel(slabs, *refs):
    pieces = refs[:PIECES]
    palette_ref, light_ref, entry_ref, exit_ref, setting_ref, span_ref, chunk_ref, staged, flanks, ready = refs[PIECES:]
    rows_piece, depth_sub, columns = pieces[0].shape
    rows_two = PIECES * rows_piece
    blocks = columns // LANES
    halves = blocks * PER
    tiles = columns // (2 * GROUP)
    flat = rows_two * depth_sub
    settle(depth_sub * tiles, palette_ref, light_ref, entry_ref, exit_ref, setting_ref, span_ref)
    sub, group, _ = places()
    lead = 32
    pick = lax.broadcasted_iota(jnp.int32, (16, LANES), 0)
    lane = lax.broadcasted_iota(jnp.int32, (16, LANES), 1)
    hit = lane == GROUP * (pick % PER) + (GROUP - 1) * (pick // PER)
    pick = jnp.where(hit, jnp.where(pick // PER == 1, -1.0, 1.0), 0.0).astype(chunk_ref.dtype)
    for block in range(blocks):
        for number, piece_ref in enumerate(pieces):
            part = piece_ref[:, :, block * LANES:(block + 1) * LANES].astype(F32)
            size = rows_piece * depth_sub
            staged[block, lead + number * size:lead + (number + 1) * size, :] = part.reshape(size, LANES)
        staged[block, lead + flat:lead + LANES, :] = jnp.zeros((LANES - flat, LANES), F32)
        whole = staged[block, lead:lead + LANES, :].astype(chunk_ref.dtype)
        turned = lax.dot_general(pick, whole, (((1,), (1,)), ((), ())), preferred_element_type=F32)
        flanks[16 * block:16 * block + 16, :] = turned

    def rows_of(block, sub_sample, row):
        return staged[block, pl.ds(lead + row * depth_sub + sub_sample, 8, stride=depth_sub), :]

    def flank(index, end):
        if index < 0 or index >= halves:
            return jnp.zeros((8, LANES), F32)
        at = 16 * (index // PER) + index % PER + PER * end
        return jnp.broadcast_to(flanks[pl.ds(at, 1), :], (8, LANES))

    for block in range(blocks):
        first = exchange([rows_of(block, s, 1) for s in range(depth_sub)], group)
        second = exchange([rows_of(block, s, 9) for s in range(depth_sub)], group)
        outer = exchange(
            [jnp.where(sub == 3, rows_of(block, s, -3), rows_of(block, s, rows_two - 1)) for s in range(depth_sub)],
            group,
        )
        for place in range(PER):
            index = block * PER + place
            tail = jnp.where(
                sub == 1, flank(index - 1, 1), jnp.where(sub == 2, flank(index + 1, 0), outer[place])
            )
            side, at = index % 2, CHUNK * (index // 2)
            ready[side, at:at + 8, :] = first[place]
            ready[side, at + 8:at + 16, :] = second[place]
            ready[side, at + 16:at + 20, :] = tail[:4]
    for side in range(2):
        for at in range(0, tiles * CHUNK, 32):
            rows = ready[side, at:at + 32, :].astype(chunk_ref.dtype)
            for slab in range(side, slabs, 2):
                start = slab * tiles * CHUNK + at
                chunk_ref[start:start + 32, :] = rows


def ray_kernel(tiles, slabs, optical_scale, setting_ref, span_ref, chunk_ref, mine_ref, other_ref, cells, slopes, wide, sides, edges):
    depth_sub = PER
    slab_len = tiles * depth_sub
    slope = [setting_ref[ch] for ch in range(3)]
    offset = [setting_ref[3 + ch] for ch in range(3)]
    light = [setting_ref[6 + axis] for axis in range(3)]
    target = [setting_ref[9], setting_ref[10]]
    scale = optical_scale * math.log2(math.e)
    sub, group, col = places()
    zero = jnp.zeros((8, LANES), F32)
    unroll = tiles <= SHORT

    def each(count, step, carry):
        if unroll:
            for index in range(count):
                carry = step(index, carry)
            return carry
        return lax.fori_loop(0, count, step, carry)

    eye = lax.broadcasted_iota(jnp.int32, (80, LANES), 0) == lax.broadcasted_iota(jnp.int32, (80, LANES), 1)
    eye = eye.astype(F32).astype(chunk_ref.dtype)
    source = lax.broadcasted_iota(jnp.int32, (LANES, LANES), 0)
    drain = lax.broadcasted_iota(jnp.int32, (LANES, LANES), 1)
    same = source // GROUP == drain // GROUP
    band = jnp.where(same & (source == drain + 1), 1.0, 0.0) - jnp.where(same & (source == drain - 1), 1.0, 0.0)
    band = band.astype(chunk_ref.dtype)
    odd = (sub % 2 == 1, (sub % 2 == 1) & (sub < 7))
    rim = (col == 0) | (col == GROUP - 1)

    def unpack(base):
        count = PER * tiles * CHUNK
        start = base * tiles * CHUNK
        step = 160

        def piece(index, nothing):
            at = index * step
            if not (isinstance(at, int) and isinstance(start, int)):
                at = pl.multiple_of(at, 32)
            wide[pl.ds(at, step), :] = chunk_ref[pl.ds(pl.multiple_of(start + at, 32), step), :].astype(F32)
            return nothing

        each(count // step, piece, 0)

    def line_up(batch, count=PER):
        for k in range(count):
            for end in range(2):
                at = (k * tiles + batch * BATCH) * CHUNK + 17 + end
                sides[pl.ds(k * GROUP + (GROUP - 1) * end, BATCH, stride=2), :] = wide[pl.ds(at, BATCH, stride=CHUNK), :]
        for part in range(2 if count == PER else 0):
            rows = slice(8 * part, 8 * part + 8)
            sides[rows, :] = jnp.where(odd[part], sides[LANES + 8 * part:LANES + 8 * part + 8, :], sides[rows, :])
        edges[...] = lax.dot_general(
            eye, sides[0:LANES, :].astype(chunk_ref.dtype), (((1,), (1,)), ((), ())), preferred_element_type=F32
        )

    def put(tile, slot):
        first, second, outer = (
            exchange([wide[pl.ds((k * tiles + tile) * CHUNK + at, 8), :] for k in range(PER)], group)
            for at in (0, 8, 12)
        )
        stack = jnp.concatenate(first + second, axis=0).astype(chunk_ref.dtype)
        inner = jnp.dot(stack, band, preferred_element_type=F32)
        for s in range(depth_sub):
            at = (tile * depth_sub + s) * UNIT
            cells[pl.ds(at, 8), :] = outer[s]
            cells[pl.ds(at + 20, 8), :] = outer[s]
            for a, here in ((0, first[s]), (1, second[s])):
                cells[pl.ds(at + 8 + 8 * a, 8), :] = here
                edge = edges[pl.ds((1 + 8 * a) * depth_sub + s, 8, stride=depth_sub), :]
                edge = turn(edge, -2 * slot) if slot else edge
                row = 8 * (PER * a + s)
                rise = inner[row:row + 8] + jnp.where(rim, edge, 0.0)
                slopes[pl.ds((tile * depth_sub + s) * 16 + 8 * a, 8), :] = rise

    def march(base, aheads, behinds, feed):
        tops = (8, 16)
        entry = [span_ref[0, 8 * half:8 * half + 8, :] - base * slab_len for half in range(2)]
        leave = [span_ref[1, 8 * half:8 * half + 8, :] - base * slab_len for half in range(2)]

        def load(half, index, shift=0):
            return cells[pl.ds(index * UNIT + tops[half] + shift, 8), :]

        def sample(half, index, after, carry):
            before, passed, prev, here, white, tinted = carry
            inside = (entry[half] <= index) & (leave[half] > index)
            excess = jnp.maximum(here - 1.5, 0.0)
            before = before - jnp.where(inside, excess * excess * scale, 0.0)
            left = jnp.exp2(before)
            rise = after - prev
            rise_row = load(half, index, 1) - load(half, index, -1)
            rise_col = slopes[pl.ds(index * 16 + 8 * half, 8), :]
            facing = rise * light[0] + rise_row * light[1] + rise_col * light[2]
            square = rise * rise + rise_row * rise_row + (rise_col * rise_col + 4.0)
            lit = (passed - left) * (0.3 + jnp.abs(facing) * lax.rsqrt(square))
            white = white + lit
            tinted = [tinted[ch] + lit * jnp.tanh(here * slope[ch] + offset[ch]) for ch in range(3)]
            return before, left, here, after, white, tinted

        def chunk(tile, carries, last=False):
            if not last:
                feed(tile + 1)
            carries = list(carries)
            for s in range(depth_sub):
                index = tile * depth_sub + s
                for half in range(2):
                    final = last and s == depth_sub - 1
                    after = behinds[half] if final else load(half, index + 1)
                    carries[half] = sample(half, index, after, carries[half])
            return carries

        carries = [
            (zero, zero + 1.0, aheads[half], load(half, 0), zero, [zero] * 3) for half in range(2)
        ]
        carries = each(tiles - 1, chunk, carries)
        carries = chunk(tiles - 1, carries, last=True)
        return [
            ([0.5 * (carry[4] + carry[5][ch]) for ch in range(3)], carry[1]) for carry in carries
        ]

    def total(cells, join):
        return join(join(cells, turn(cells, GROUP)), join(turn(cells, 2 * GROUP), turn(cells, 3 * GROUP)))

    def over(base, half, colour, passed, state):
        reached, layers = state
        before = reached
        for step in range(1, PER):
            before = before * jnp.where(group >= step, turn(passed, step * GROUP), 1.0)
        where = (group + base).astype(F32)
        result = []
        for place, (sums, through) in zip(target, layers):
            keep = where <= place
            sums = [sums[ch] + total(jnp.where(keep, before * colour[ch], 0.0), jnp.add) for ch in range(3)]
            through = through * total(jnp.where(keep, passed, 1.0), jnp.multiply)
            result.append((sums, through))
        return reached * total(passed, jnp.multiply), result

    def four(index, states):
        base = index * PER
        end = slab_len - 1
        unpack(base)
        if unroll:
            line_up(0)
            put(tiles - 1, tiles - 1)
            put(0, 0)
        else:

            def batch(number, nothing):
                line_up(number)
                for slot in range(BATCH):
                    put(number * BATCH + slot, slot)
                return nothing

            lax.fori_loop(0, tiles // BATCH, batch, 0)
        rolled, aheads, behinds = [], [], []
        for half in range(2):
            top = 8 + 8 * half
            rolled.append(turn(cells[pl.ds(end * UNIT + top, 8), :], GROUP))
            aheads.append(jnp.where(group == 0, states[half][0], rolled[half]))
            start = turn(cells[pl.ds(top, 8), :], -GROUP)
            if isinstance(index, int) and base + PER >= slabs:
                beyond = zero
            else:
                following = jnp.minimum(base + PER, slabs - PER)
                at = pl.multiple_of(following * (tiles * CHUNK), 32)
                raw = chunk_ref[pl.ds(at, 16), :].astype(F32)[8 * half:8 * half + 8]
                beyond = jnp.where(base + PER < slabs, turn(raw, -GROUP), zero)
            behinds.append(jnp.where(group == PER - 1, beyond, start))

        def feed(tile):
            if unroll and tile < tiles - 1:
                put(tile, tile)

        found = march(base, aheads, behinds, feed)
        return [
            (rolled[half], over(base, half, *found[half], states[half][1])) for half in range(2)
        ]

    def deep():
        empty = (zero + 1.0, [([zero] * 3, zero + 1.0) for _ in range(2)])
        states = [(zero, empty) for _ in range(2)]
        if slabs == PER:
            states = four(0, states)
        else:
            states = lax.fori_loop(0, slabs // PER, four, states)
        for half in range(2):
            _, (_, layers) = states[half]
            for ref, (sums, through) in zip((mine_ref, other_ref), layers):
                for ch, value in enumerate((*sums, through)):
                    ref[ch, 8 * half:8 * half + 8, :] = value

    def shallow():
        for at in range(0, 2 * tiles * CHUNK + 16, 16):
            wide[at:at + 16, :] = chunk_ref[at:at + 16, :].astype(F32)
        line_up(0, 2)
        end = slab_len - 1

        def place(tile):
            def swap(at):
                return exchange(
                    [wide[pl.ds((k * tiles + tile) * CHUNK + at[a], 8), :] for a in range(2) for k in range(2)], group
                )

            centre, below, above = swap((0, 8)), swap((1, 9)), swap((12, 0))
            stack = jnp.concatenate(centre, axis=0).astype(chunk_ref.dtype)
            inner = jnp.dot(stack, band, preferred_element_type=F32)
            for s in range(depth_sub):
                at = (tile * depth_sub + s) * UNIT
                cells[pl.ds(at, 8), :] = above[s]
                cells[pl.ds(at + 9, 8), :] = below[s]
                cells[pl.ds(at + 8, 8), :] = centre[s]
                edge = [edges[pl.ds((1 + 8 * a) * depth_sub + s, 8, stride=depth_sub), :] for a in range(2)]
                edge = jnp.where(group < 2, turn(edge[0], -2 * tile), turn(edge[1], 2 * GROUP - 2 * tile))
                rise = inner[8 * s:8 * s + 8] + jnp.where(rim, edge, 0.0)
                slopes[pl.ds((tile * depth_sub + s) * 16, 8), :] = rise

        for tile in range(tiles):
            place(tile)

        def load(index, shift=0):
            return cells[pl.ds(index * UNIT + 8 + shift, 8), :]

        def span(which):
            return jnp.where(group < 2, span_ref[which, 0:8, :], turn(span_ref[which, 8:16, :], 2 * GROUP))

        entry, leave = span(0), span(1)
        odd_group = group % 2 == 1
        beyond = [wide[pl.ds(2 * tiles * CHUNK + 8 * a, 8), :] for a in range(2)]
        beyond = jnp.where(group < 2, turn(beyond[0], GROUP), turn(beyond[1], 3 * GROUP))
        behind = jnp.where(odd_group, beyond, turn(load(0), -GROUP))
        prev = jnp.where(odd_group, turn(load(end), GROUP), 0.0)
        here, before, passed, white, tinted = load(0), zero, zero + 1.0, zero, [zero] * 3
        for index in range(slab_len):
            after = behind if index == end else load(index + 1)
            inside = (entry <= index) & (leave > index)
            excess = jnp.maximum(here - 1.5, 0.0)
            before = before - jnp.where(inside, excess * excess * scale, 0.0)
            left = jnp.exp2(before)
            rise = after - prev
            rise_row = load(index, 1) - load(index, -1)
            rise_col = slopes[pl.ds(index * 16, 8), :]
            facing = rise * light[0] + rise_row * light[1] + rise_col * light[2]
            square = rise * rise + rise_row * rise_row + (rise_col * rise_col + 4.0)
            lit = (passed - left) * (0.3 + jnp.abs(facing) * lax.rsqrt(square))
            white = white + lit
            tinted = [tinted[ch] + lit * jnp.tanh(here * slope[ch] + offset[ch]) for ch in range(3)]
            passed, prev, here = left, here, after
        reached = jnp.where(odd_group, turn(passed, GROUP), 1.0)
        where = (group % 2).astype(F32)
        for goal, ref in zip(target, (mine_ref, other_ref)):
            keep = where <= goal
            parts = [jnp.where(keep, reached * (0.5 * (white + tinted[ch])), 0.0) for ch in range(3)]
            for ch, value in enumerate((*parts, jnp.where(keep, passed, 1.0))):
                join = jnp.multiply if ch == 3 else jnp.add
                value = join(value, jnp.where(odd_group, turn(value, GROUP), turn(value, -GROUP)))
                ref[ch, 0:8, :] = value
                ref[ch, 8:16, :] = turn(value, 2 * GROUP)

    if slabs == PER and unroll:
        near = lax.axis_index("depth") < 2
        pl.when(near)(shallow)
        pl.when(jnp.logical_not(near))(deep)
    else:
        deep()


def join_kernel(setting_ref, mine_ref, other_ref, out_ref):
    _, group, _ = places()
    own = (group == 1) == (setting_ref[11] > 0.5)
    for half in range(2):
        rows = slice(8 * half, 8 * half + 8)
        for ch in range(4):
            both = jnp.where(own, mine_ref[ch, rows, :], other_ref[ch, rows, :])
            out_ref[0, ch, rows, :] = both[:, :2 * GROUP]


def body(volume, ray_entry, ray_exit, palette, light_dir):
    tiles = lax.axis_size("tile")
    slabs = lax.axis_size("depth")
    depth_sub, rows_two, columns = volume.shape
    rows, col_dev = ray_entry.shape
    slab_len = depth_sub * tiles
    devices = tiles * slabs
    small = devices <= 64
    vmem = pl.BlockSpec(memory_space=VMEM)
    resident = functools.partial(pltpu.with_memory_space_constraint, memory_space=VMEM)
    smem = pl.BlockSpec(memory_space=pltpu.SMEM)
    chunks_shape = (devices * CHUNK, LANES)

    cells = jnp.transpose(volume, (1, 0, 2))
    shape = (rows_two // PIECES, depth_sub, columns)
    windows = [pl.BlockSpec(shape, functools.partial(lambda piece, _: (piece, 0, 0), piece)) for piece in range(PIECES)]
    setting, span, chunks = pl.pallas_call(
        functools.partial(pack_kernel, slabs),
        out_shape=[
            pltpu.VMEM((12, 8, LANES), F32),
            pltpu.VMEM((2, rows, LANES), jnp.int32),
            (pltpu.VMEM if small else jax.ShapeDtypeStruct)(chunks_shape, volume.dtype),
        ],
        grid=(1,),
        in_specs=windows + [smem] * 2 + [vmem] * 2,
        out_specs=[vmem] * 3,
        scratch_shapes=[
            pltpu.VMEM((columns // LANES, 160, LANES), F32),
            pltpu.VMEM((16 * (columns // LANES), LANES), F32),
            pltpu.VMEM((2, tiles * CHUNK, LANES), F32),
        ],
        name="pack",
    )(*[cells] * PIECES, palette.T, light_dir, ray_entry, ray_exit)
    chunks = chunks.reshape(devices, CHUNK // 4, 4, LANES)
    chunks = lax.all_to_all(chunks, ("depth", "tile"), split_axis=0, concat_axis=0, tiled=True)
    chunks = chunks.reshape(devices * CHUNK, LANES)
    mine, other = pl.pallas_call(
        functools.partial(ray_kernel, tiles, slabs, 64.0 / (slab_len * slabs)),
        out_shape=[pltpu.VMEM((4, rows, LANES), F32)] * 2,
        in_specs=[vmem] * 3,
        out_specs=[vmem] * 2,
        scratch_shapes=[
            pltpu.VMEM((slab_len * UNIT, LANES), F32),
            pltpu.VMEM((slab_len * 16, LANES), F32),
            pltpu.VMEM((PER * tiles * CHUNK + 32, LANES), F32),
            pltpu.VMEM((LANES + 16, LANES), F32),
            pltpu.VMEM((80, LANES), F32),
        ],
        name="ray",
    )(resident(setting), resident(span), resident(chunks) if small else chunks)
    other = lax.ppermute(other, "depth", [(i, i ^ 1) for i in range(slabs)])
    return pl.pallas_call(
        join_kernel,
        out_shape=jax.ShapeDtypeStruct((1, 4, rows, col_dev), F32),
        in_specs=[vmem] * 3,
        out_specs=vmem,
        name="join",
    )(resident(setting), resident(mine), resident(other))


def solution(mesh):
    return jax.shard_map(
        body,
        mesh=mesh,
        in_specs=(P(("depth", "tile"), None, None), P(None, "tile"), P(None, "tile"), P(), P()),
        out_specs=P("depth", None, None, "tile"),
        check_vma=False,
    )
```
